128 devices in a mesh: frames: 16 (over y, x_lo, core), tiles: 8 (over x_hi, z).
Axes of the slice: x: 4 (x_hi: 2, x_lo: 2; x = x_hi * 2 + x_lo), y: 4, z: 4, core: 2. Of those that a mesh axis runs over, the one named last changes fastest.
Arguments:
- raw: bfloat16 [128, 8, 512, 1024], P('frames', None, None, 'tiles'), may hold values from -6 to 6
- offsets: int32 [128, 3], P('frames'), may hold values from -3 to 3
- taps: float32 [64], replicated, may hold values from -0.75 to 0.75
Outputs:
- activity: bfloat16 [128, 8, 512, 1024], P(None, None, 'frames', 'tiles')
- template: float32 [8, 512, 1024], P(None, 'frames', 'tiles')
The draws below stay inside these ranges and needn't reach their ends.
All inputs are finite; a program needn't handle non-finite values.
Results may differ from the reference program's by a relative error of at most 0.006.
Values may be sent and summed in bfloat16 or wider, within the bound.
No kernel may reach another device: no remote copies, remote signals or barrier semaphores. Data moves between devices by JAX's collectives and lax.ppermute only.
A program may use at most 192 MiB of HBM per device.

```python
import jax
import jax.numpy as jnp
from jax import lax

Z = 8
Y = 512
TAPS = 64
SHIFT = 3
RADIUS = 8
FRAMES = 128
X = 1024


def set_ends(values, rng, least, largest):
    index_at = [jax.random.randint(jax.random.fold_in(rng, axis), (), 0, length) for axis, length in enumerate(values.shape)]
    longest = values.shape.index(max(values.shape))
    beside = index_at[:longest] + [(index_at[longest] + 1) % values.shape[longest]] + index_at[longest + 1:]
    return values.at[tuple(index_at)].set(least).at[tuple(beside)].set(largest)


def block_levels(rng, extent, pieces, smallest, high):
    factor_of = 1.0
    for dim, shards_of in pieces:
        steps = jax.random.uniform(jax.random.fold_in(jax.random.fold_in(rng, 6), dim), (shards_of,), jnp.float32, smallest / len(pieces), high / len(pieces))
        factor_of = factor_of * jnp.repeat(jnp.exp(steps), extent[dim] // shards_of).reshape((-1,) + (1,) * (len(extent) - 1 - dim))
    return factor_of


def bell_draw(key, extent, deviation, reach, shards=(), held_as=jnp.bfloat16):
    drawn = jax.random.normal(key, extent, jnp.float32) * deviation
    if len(shards) > 0:
        drawn = block_levels(key, extent, shards, -0.22, 0.18) * drawn
    return jnp.clip(drawn, min=-reach, max=reach).astype(held_as)


def setup_inputs(seed: int = 0) -> dict:
    arg_keys = jax.random.split(jax.random.key(seed), 4)
    raw = bell_draw(arg_keys[0], (FRAMES, Z, Y, X), 1.0, 6.0, ((0, 16), (3, 8)))
    offsets = set_ends(jax.random.randint(arg_keys[1], (FRAMES, 3), 0 - SHIFT, SHIFT + 1), jax.random.fold_in(arg_keys[1], 1), 0 - SHIFT, SHIFT).astype(jnp.int32)
    taps = bell_draw(arg_keys[2], (TAPS,), TAPS ** -0.5, 0.75, (), jnp.float32)
    return {"raw": raw, "offsets": offsets, "taps": taps}


def smooth_axis(volume, axis):
    count = volume.shape[axis]
    widths = [(0, 0)] * volume.ndim
    widths[axis] = (1, 1)
    padded = jnp.pad(volume, widths)
    lower = lax.slice_in_dim(padded, 0, count, axis=axis)
    middle = lax.slice_in_dim(padded, 1, count + 1, axis=axis)
    upper = lax.slice_in_dim(padded, 2, count + 2, axis=axis)
    return (lower + 2.0 * middle + upper) * 0.25


def reference(raw, offsets, taps):
    positions = jnp.arange(Y, dtype=jnp.int32)
    band_ones = (jnp.abs(positions[:, None] - positions[None, :]) <= RADIUS).astype(jnp.float32)

    def register(summed, inputs):
        frame, offset = inputs
        wide = frame.astype(jnp.float32)
        box = jnp.einsum('zyx,yw->zwx', wide, band_ones)
        highpass = wide - box / (2 * RADIUS + 1)
        padded = jnp.pad(highpass, ((SHIFT, SHIFT), (SHIFT, SHIFT), (SHIFT, SHIFT)))
        starts = (SHIFT - offset[0]).astype(jnp.int32), (SHIFT - offset[1]).astype(jnp.int32), (SHIFT - offset[2]).astype(jnp.int32)
        shifted = lax.dynamic_slice(padded, starts, (Z, Y, X))
        return summed + shifted, shifted.astype(jnp.bfloat16)

    summed, moved = lax.scan(register, jnp.zeros((Z, Y, X), jnp.float32), (raw, offsets))
    template = summed / FRAMES
    frame_index = jnp.arange(FRAMES, dtype=jnp.int32)
    lag_index = frame_index[:, None] - frame_index[None, :]
    valid = (lag_index >= 0) & (lag_index < TAPS)
    toeplitz = jnp.where(valid, taps[jnp.clip(lag_index, 0, TAPS - 1)], 0.0).astype(jnp.bfloat16)
    rowsum = jnp.sum(toeplitz.astype(jnp.float32), axis=1)
    planes = []
    for plane in range(Z):
        flat = moved[:, plane].reshape(FRAMES, Y * X)
        product = jnp.dot(toeplitz, flat, preferred_element_type=jnp.float32).reshape(FRAMES, Y, X)
        filtered = product - rowsum[:, None, None] * template[plane][None]
        planes.append(smooth_axis(smooth_axis(filtered, 1), 2))
    outputs = []
    for plane in range(Z):
        lower = planes[plane - 1] if plane > 0 else jnp.zeros_like(planes[0])
        upper = planes[plane + 1] if plane + 1 < Z else jnp.zeros_like(planes[0])
        outputs.append(((lower + 2.0 * planes[plane] + upper) * 0.25).astype(jnp.bfloat16))
    activity = jnp.stack(outputs, axis=1)
    return activity, template
```

```python
import jax
import jax.numpy as jnp
from jax import lax
from jax.experimental import pallas as pl
from jax.experimental.pallas import tpu as pltpu
from jax.sharding import PartitionSpec as P

TAPS = 64
SHIFT = 3
RADIUS = 8
HALO = SHIFT + 1
BOX = 2 * RADIUS + 1
LANES = 128
SUB = 8
CHUNKS = (2, 2, 2, 2)
PACK = LANES // (8 * HALO)
VMEM = 56 << 20


def iota(shape, dim):
    return lax.broadcasted_iota(jnp.int32, shape, dim)


def dot(a, b):
    return jnp.dot(a, b, preferred_element_type=jnp.float32)


def pack_body(raw_ref, first_ref, last_ref):
    slot = lax.rem(pl.program_id(0), PACK)
    planes, rows, lanes = raw_ref.shape[1:]
    source = iota((planes * lanes, 2 * LANES), 0)
    target = iota((planes * lanes, 2 * LANES), 1)
    plane, column = source // lanes, source % lanes
    side, lane = target // LANES, target % LANES
    column = column - side * (lanes - HALO)
    wanted = slot * planes * HALO + plane * HALO + column
    pick = ((lane == wanted) & (column >= 0) & (column < HALO)).astype(jnp.float32).astype(jnp.bfloat16)
    wide = jnp.concatenate([raw_ref[0, z] for z in range(planes)], axis=1)
    edges = dot(wide, pick).astype(jnp.bfloat16)

    @pl.when(slot == 0)
    def _():
        first_ref[0] = edges[:, :LANES]
        last_ref[0] = edges[:, LANES:]

    @pl.when(slot != 0)
    def _():
        first_ref[0] += edges[:, :LANES]
        last_ref[0] += edges[:, LANES:]


def pack_edges(raw):
    frames, planes, rows, lanes = raw.shape
    groups = frames // PACK
    edge = jax.ShapeDtypeStruct((groups, rows, LANES), jnp.bfloat16)
    spec = pl.BlockSpec((1, rows, LANES), lambda f: (f // PACK, 0, 0))
    return pl.pallas_call(
        pack_body,
        grid=(frames,),
        in_specs=[pl.BlockSpec((1, planes, rows, lanes), lambda f: (f, 0, 0, 0))],
        out_specs=(spec, spec),
        out_shape=(edge, edge),
        compiler_params=pltpu.CompilerParams(vmem_limit_bytes=VMEM),
        name="pack_edges",
    )(raw)


def register_body(first, count, total, last, meta_ref, raw_ref, left_ref, right_ref, *rest):
    if first > 0:
        sum_in_ref, *rest = rest
    send_ref, *rest = rest
    if not last:
        sum_out_ref, *rest = rest
    matrix, table, edge_table, smooth, summed = rest
    planes, rows, lanes = raw_ref.shape[1:]
    blocks = send_ref.shape[0]
    strip = rows // blocks
    step = pl.program_id(0)

    @pl.when(step == 0)
    def _():
        smooth[0:HALO] = jnp.zeros((HALO, rows, lanes), jnp.float32)
        smooth[HALO + planes :] = jnp.zeros((HALO, rows, lanes), jnp.float32)
        if first > 0:
            summed[SHIFT : SHIFT + planes] = sum_in_ref[...]
        else:
            summed[SHIFT : SHIFT + planes] = jnp.zeros((planes, rows, lanes), jnp.float32)

    def frame():
        index = first + step
        off_z, off_y, off_x = meta_ref[3 * index], meta_ref[3 * index + 1], meta_ref[3 * index + 2]
        at_start, at_end = meta_ref[3 * total], meta_ref[3 * total + 1]

        def fill(block, carry):
            base = pl.multiple_of(block * 64, 64)
            out_row = iota((64, rows), 0) + base
            in_row = iota((64, rows), 1)
            value = jnp.zeros((64, rows), jnp.float32)
            for delta, weight in ((-1, 1.0), (1, 1.0), (0, 2.0)):
                reached = out_row + delta
                source = reached - off_y
                inside = (reached >= 0) & (reached < rows) & (source >= 0) & (source < rows)
                gap = jnp.abs(in_row - source)
                term = jnp.where(gap == 0, BOX - 1.0, jnp.where(gap <= RADIUS, -1.0, 0.0))
                term = jnp.where(inside, term, 0.0)
                value = value + weight * term
                if delta == 0:
                    matrix[pl.ds(rows + base, 64), :] = term.astype(jnp.bfloat16)
            matrix[pl.ds(base, 64), :] = value.astype(jnp.bfloat16)
            return carry

        lax.fori_loop(0, rows // 64, fill, 0)
        both = matrix[...]

        slot = lax.rem(index, PACK)
        source = iota((2 * LANES, LANES), 0)
        target = iota((2 * LANES, LANES), 1)
        side, lane = source // LANES, source % LANES - slot * planes * HALO
        plane, column = lane // HALO, lane % HALO
        chosen = (lane >= 0) & (lane < planes * HALO) & (target == plane * 2 * HALO + side * HALO + column)
        pick = chosen.astype(jnp.float32).astype(jnp.bfloat16)
        edges = dot(jnp.concatenate([left_ref[0], right_ref[0]], axis=1), pick).astype(jnp.bfloat16)
        edge_table[...] = dot(both, edges)

        column = iota((strip, lanes), 1)
        weight_low = jnp.where((column == 0) & (at_start > 0), 0.0, 1.0)
        weight_high = jnp.where((column == lanes - 1) & (at_end > 0), 0.0, 1.0)
        within = {d: (column + d - off_x >= 0) & (column + d - off_x < lanes) for d in (-1, 0, 1)}

        for pair in range(planes // 2):
            table[...] = dot(both, jnp.concatenate([raw_ref[0, 2 * pair], raw_ref[0, 2 * pair + 1]], axis=1))

            def across(block, carry, pair=pair):
                low = pl.multiple_of(block * strip, strip)
                for half in range(2):
                    z = 2 * pair + half
                    base = 2 * HALO * z + HALO

                    def moved(start, delta):
                        body = table[pl.ds(start, strip), half * lanes : (half + 1) * lanes]
                        edge = edge_table[pl.ds(start, strip), :]
                        by = off_x - delta
                        return jnp.where(
                            within[delta],
                            pltpu.roll(body, (by + lanes) & (lanes - 1), 1),
                            pltpu.roll(edge, (by - base + 2 * lanes) & (lanes - 1), 1),
                        )

                    smoothed = weight_low * moved(low, -1) + 2.0 * moved(low, 0) + weight_high * moved(low, 1)
                    smooth[HALO + z, pl.ds(low, strip), :] = smoothed
                    summed[SHIFT + z + off_z, pl.ds(low, strip), :] += moved(rows + low, 0)
                return carry

            lax.fori_loop(0, blocks, across, 0)

        def along(block, carry):
            low = pl.multiple_of(block * strip, strip)
            plane = [smooth[HALO + z - off_z, pl.ds(low, strip), :] for z in range(planes)]
            for z in range(planes):
                value = 2.0 * plane[z]
                if z > 0:
                    value = value + plane[z - 1]
                if z + 1 < planes:
                    value = value + plane[z + 1]
                send_ref[block, 0, z] = (value * (1.0 / (BOX * 64))).astype(jnp.bfloat16)
            return carry

        lax.fori_loop(0, blocks, along, 0)

    if not last:
        frame()

        @pl.when(step == count - 1)
        def _():
            sum_out_ref[...] = summed[SHIFT : SHIFT + planes]
    else:
        pl.when(step < count)(frame)

        @pl.when(step == count)
        def _():
            def hand(block, carry):
                low = pl.multiple_of(block * strip, strip)
                for z in range(planes):
                    send_ref[block, 0, z] = (summed[SHIFT + z, pl.ds(low, strip), :] * (1.0 / BOX)).astype(jnp.bfloat16)
                return carry

            lax.fori_loop(0, blocks, hand, 0)


def register(raw, left, right, meta, summed, first, count, owners, last):
    frames, planes, rows, lanes = raw.shape
    steps = count + 1 if last else count

    def at(f):
        return first + jnp.minimum(f, count - 1)

    edge_spec = pl.BlockSpec((1, rows, LANES), lambda f, m: (at(f) // PACK, 0, 0))
    whole = pl.BlockSpec((planes, rows, lanes), lambda f, m: (0, 0, 0))
    in_specs = [pl.BlockSpec((1, planes, rows, lanes), lambda f, m: (at(f), 0, 0, 0)), edge_spec, edge_spec]
    operands = [raw, left, right]
    if first > 0:
        in_specs.append(whole)
        operands.append(summed)
    strip = rows // owners
    out_specs = [pl.BlockSpec((owners, 1, planes, strip, lanes), lambda f, m: (0, f, 0, 0, 0))]
    out_shape = [jax.ShapeDtypeStruct((owners, steps, planes, strip, lanes), jnp.bfloat16)]
    if not last:
        out_specs.append(whole)
        out_shape.append(jax.ShapeDtypeStruct((planes, rows, lanes), jnp.float32))

    def body(*refs):
        register_body(first, count, frames, last, *refs)

    return pl.pallas_call(
        body,
        grid_spec=pltpu.PrefetchScalarGridSpec(
            num_scalar_prefetch=1,
            grid=(steps,),
            in_specs=in_specs,
            out_specs=tuple(out_specs),
            scratch_shapes=[
                pltpu.VMEM((2 * rows, rows), jnp.bfloat16),
                pltpu.VMEM((2 * rows, 2 * lanes), jnp.float32),
                pltpu.VMEM((2 * rows, LANES), jnp.float32),
                pltpu.VMEM((planes + 2 * HALO, rows, lanes), jnp.float32),
                pltpu.VMEM((planes + 2 * SHIFT, rows, lanes), jnp.float32),
            ],
        ),
        out_shape=tuple(out_shape),
        compiler_params=pltpu.CompilerParams(vmem_limit_bytes=VMEM),
        name=f"register_{first}",
    )(meta, *operands)


def spread_body(taps_ref, order_ref, kernel_ref, rowsum_ref):
    total = order_ref.shape[1]
    frame = iota((total, total), 0)
    lag = frame - jnp.broadcast_to(order_ref[0:1, :], (total, total))
    value = jnp.zeros((total, total), jnp.float32)
    for tap in range(TAPS):
        value = jnp.where(lag == tap, taps_ref[tap], value)
    small = value.astype(jnp.bfloat16)
    rowsum = jnp.sum(small.astype(jnp.float32), axis=1, keepdims=True) * (1.0 / total)
    rowsum_ref[...] = jnp.broadcast_to(rowsum[:, :, None], (total, SUB, LANES)).reshape(total * SUB, LANES)
    repeat = iota((total, total * SUB), 1) // SUB == iota((total, total * SUB), 0)
    wide = dot(small, repeat.astype(jnp.float32).astype(jnp.bfloat16))
    tall = jnp.broadcast_to(wide[:, None, :], (total, SUB, total * SUB)).reshape(total * SUB, total * SUB)
    same = iota(tall.shape, 0) % SUB == iota(tall.shape, 1) % SUB
    kernel_ref[...] = jnp.where(same, tall, 0.0).astype(jnp.bfloat16)


def spread_kernel(taps, order):
    total = order.shape[1]
    return pl.pallas_call(
        spread_body,
        in_specs=[pl.BlockSpec(memory_space=pltpu.SMEM), pl.BlockSpec(memory_space=pltpu.VMEM)],
        out_shape=(
            jax.ShapeDtypeStruct((total * SUB, total * SUB), jnp.bfloat16),
            jax.ShapeDtypeStruct((total * SUB, LANES), jnp.float32),
        ),
        compiler_params=pltpu.CompilerParams(vmem_limit_bytes=VMEM),
        name="spread_kernel",
    )(taps, order)


def filter_body(group, kernel_ref, rowsum_ref, *refs):
    *got, out_ref, template_ref = refs
    owners = got[0].shape[0]
    total, _, strip, lanes = out_ref.shape
    frames = group * (total // owners)
    width = frames * SUB
    reach = -(-TAPS // frames)

    sent = got[-1][:, CHUNKS[-1], 0].astype(jnp.float32)
    template_ref[0] = jnp.sum(sent, axis=0) * (1.0 / total)

    for pair in range(strip // (2 * SUB)):
        tiles = []
        for j in range(owners // group):
            halves = []
            for half in range(2):
                low = (2 * pair + half) * SUB
                parts = []
                for ref, count in zip(got, CHUNKS):
                    part = ref[group * j : group * (j + 1), 0:count, 0, low : low + SUB, :]
                    parts.append(part.reshape(group * count * SUB, lanes))
                halves.append(jnp.concatenate(parts, axis=0))
            tiles.append(jnp.concatenate(halves, axis=1))
        mean = sum(jnp.sum(t.astype(jnp.float32).reshape(frames, SUB, 2 * lanes), axis=0) for t in tiles)
        for i in range(len(tiles)):
            lowest = max(0, i - reach)
            rows = slice(i * width, (i + 1) * width)
            value = None
            for j in range(lowest, i + 1):
                part = dot(kernel_ref[rows, j * width : (j + 1) * width], tiles[j])
                value = part if value is None else value + part
            rowsum = rowsum_ref[rows, :].reshape(frames, SUB, lanes)
            value = value.reshape(frames, SUB, 2 * lanes)
            done = [
                value[:, :, h * lanes : (h + 1) * lanes] - rowsum * mean[None, :, h * lanes : (h + 1) * lanes]
                for h in range(2)
            ]
            both = jnp.concatenate(done, axis=1).astype(jnp.bfloat16)
            out_ref[i * frames : (i + 1) * frames, 0, 2 * SUB * pair : 2 * SUB * (pair + 1), :] = both


def filter_frames(kernel, rowsum, got, total, group):
    owners, _, planes, strip, lanes = got[0].shape
    in_specs = [
        pl.BlockSpec(kernel.shape, lambda z: (0, 0)),
        pl.BlockSpec(rowsum.shape, lambda z: (0, 0)),
    ]
    for part in got:
        in_specs.append(pl.BlockSpec((owners, part.shape[1], 1, strip, lanes), lambda z: (0, 0, z, 0, 0)))

    def body(*refs):
        filter_body(group, *refs)

    return pl.pallas_call(
        body,
        grid=(planes,),
        in_specs=in_specs,
        out_specs=(
            pl.BlockSpec((total, 1, strip, lanes), lambda z: (0, z, 0, 0)),
            pl.BlockSpec((1, strip, lanes), lambda z: (z, 0, 0)),
        ),
        out_shape=(
            jax.ShapeDtypeStruct((total, planes, strip, lanes), jnp.bfloat16),
            jax.ShapeDtypeStruct((planes, strip, lanes), jnp.float32),
        ),
        compiler_params=pltpu.CompilerParams(vmem_limit_bytes=VMEM),
        name="filter_frames",
    )(kernel, rowsum, *got)


def local(raw, offsets, taps):
    frame_dev, planes, rows, lanes = raw.shape
    owners = lax.axis_size("frames")
    tiles = lax.axis_size("tiles")
    total = frame_dev * owners
    group = min(owners, 4)

    first_columns, last_columns = pack_edges(raw)
    upward = [(i, i + 1) for i in range(tiles - 1)]
    left = lax.ppermute(last_columns, "tiles", upward)
    right = lax.ppermute(first_columns, "tiles", [(j, i) for i, j in upward])

    tile = lax.axis_index("tiles")
    ends = jnp.stack([tile == 0, tile == tiles - 1]).astype(jnp.int32)
    meta = jnp.concatenate([offsets.reshape(-1), ends])

    order = []
    for block in range(owners // group):
        low = 0
        for count in CHUNKS:
            for owner in range(group * block, group * (block + 1)):
                order += [owner * frame_dev + low + f for f in range(count)]
            low += count
    kernel, rowsum = spread_kernel(taps, jnp.tile(jnp.array(order, jnp.int32)[None], (SUB, 1)))

    got = []
    summed = None
    low = 0
    for number, count in enumerate(CHUNKS):
        is_last = number == len(CHUNKS) - 1
        made = register(raw, left, right, meta, summed, low, count, owners, is_last)
        if not is_last:
            summed = made[1]
        got.append(lax.all_to_all(made[0], "frames", split_axis=0, concat_axis=0, tiled=True))
        low += count
    return filter_frames(kernel, rowsum, got, total, group)


def solution(mesh):
    placed = (P("frames", None, None, "tiles"), P("frames", None), P())
    return jax.shard_map(
        local,
        mesh=mesh,
        in_specs=placed,
        out_specs=(P(None, None, "frames", "tiles"), P(None, "frames", "tiles")),
        check_vma=False,
    )
```

```python
import jax
import jax.numpy as jnp
from jax import lax
from jax.experimental import pallas as pl
from jax.experimental.pallas import tpu as pltpu
from jax.sharding import PartitionSpec as P

TAPS = 64
SHIFT = 3
RADIUS = 8
HALO = SHIFT + 1
BOX = 2 * RADIUS + 1
LANES = 128
SUB = 8
CHUNKS = (2, 6)
PACK = LANES // (8 * HALO)
VMEM = 56 << 20


def iota(shape, dim):
    return lax.broadcasted_iota(jnp.int32, shape, dim)


def dot(a, b):
    return jnp.dot(a, b, preferred_element_type=jnp.float32)


def pack_body(*refs):
    *raw_refs, first_ref, last_ref, pick = refs
    step = pl.program_id(0)
    planes, rows, lanes = raw_refs[0].shape[1:]
    half = lax.rem(step, PACK // len(raw_refs))

    @pl.when(step == 0)
    def _():
        pick[...] = jnp.zeros(pick.shape, pick.dtype)

    low, lane = iota((SUB, LANES), 0), iota((SUB, LANES), 1)
    wide = []
    for f, raw_ref in enumerate(raw_refs):
        for z in range(planes):
            start = ((half * len(raw_refs) + f) * planes + z) * HALO
            head = (low < HALO) & (lane == start + low)
            tail = (low >= SUB - HALO) & (lane == start + low - (SUB - HALO))
            row = (f * planes + z) * lanes
            pick[row : row + SUB, :LANES] = head.astype(jnp.float32).astype(jnp.bfloat16)
            pick[row + lanes - SUB : row + lanes, LANES:] = tail.astype(jnp.float32).astype(jnp.bfloat16)
            wide.append(raw_ref[0, z])
    edges = dot(jnp.concatenate(wide, axis=1), pick[...]).astype(jnp.bfloat16)

    @pl.when(half == 0)
    def _():
        first_ref[0] = edges[:, :LANES]
        last_ref[0] = edges[:, LANES:]

    @pl.when(half != 0)
    def _():
        first_ref[0] += edges[:, :LANES]
        last_ref[0] += edges[:, LANES:]


def pack_edges(raw):
    frames, planes, rows, lanes = raw.shape
    each = 2
    edge = jax.ShapeDtypeStruct((frames // PACK, rows, LANES), jnp.bfloat16)
    spec = pl.BlockSpec((1, rows, LANES), lambda i: (i * each // PACK, 0, 0))
    return pl.pallas_call(
        pack_body,
        grid=(frames // each,),
        in_specs=[
            pl.BlockSpec((1, planes, rows, lanes), lambda i, f=f: (i * each + f, 0, 0, 0)) for f in range(each)
        ],
        out_specs=(spec, spec),
        out_shape=(edge, edge),
        scratch_shapes=[pltpu.VMEM((each * planes * lanes, 2 * LANES), jnp.bfloat16)],
        compiler_params=pltpu.CompilerParams(vmem_limit_bytes=VMEM),
        name="pack_edges",
    )(*[raw] * each)


def high_pass(out_row, in_row, off_y, rows):
    smoothed = 0.0
    for delta, weight in ((-1, 1.0), (1, 1.0), (0, 2.0)):
        reached = out_row + delta
        source = reached - off_y
        inside = (reached >= 0) & (reached < rows) & (source >= 0) & (source < rows)
        gap = jnp.abs(in_row - source)
        term = jnp.where(gap == 0, BOX - 1.0, jnp.where(gap <= RADIUS, -1.0, 0.0))
        term = jnp.where(inside, term, 0.0)
        smoothed = smoothed + weight * term
    return smoothed, term


def high_pass_inside(out_row, in_row, off_y):
    gap = jnp.abs(in_row - out_row + off_y)
    plain = jnp.where(gap == 0, BOX - 1.0, jnp.where(gap <= RADIUS, -1.0, 0.0))
    far = jnp.where(gap <= RADIUS - 1, -4.0, jnp.where(gap == RADIUS, -3.0, jnp.where(gap == RADIUS + 1, -1.0, 0.0)))
    smoothed = jnp.where(gap == 0, 2.0 * BOX - 4.0, jnp.where(gap == 1, BOX - 4.0, far))
    return smoothed, plain


def register_body(first, count, total, last, meta_ref, raw_ref, left_ref, right_ref, *rest):
    if first > 0:
        sum_in_ref, *rest = rest
    send_ref, *rest = rest
    if not last:
        sum_out_ref, *rest = rest
    smooth_y, plain_y, split, plain, smooth, summed = rest
    planes, rows, lanes = raw_ref.shape[1:]
    blocks = send_ref.shape[0]
    strip = rows // blocks
    step = pl.program_id(0)

    @pl.when(step == 0)
    def _():
        smooth_y[...] = jnp.zeros(smooth_y.shape, smooth_y.dtype)
        plain_y[...] = jnp.zeros(plain_y.shape, plain_y.dtype)
        smooth[0:HALO] = jnp.zeros((HALO, rows, lanes), jnp.float32)
        smooth[HALO + planes :] = jnp.zeros((HALO, rows, lanes), jnp.float32)
        if first > 0:
            summed[SHIFT : SHIFT + planes] = sum_in_ref[...]
        else:
            summed[SHIFT : SHIFT + planes] = jnp.zeros((planes, rows, lanes), jnp.float32)

    def frame():
        index = first + step
        off_z, off_y, off_x = meta_ref[3 * index], meta_ref[3 * index + 1], meta_ref[3 * index + 2]
        at_start, at_end = meta_ref[3 * total], meta_ref[3 * total + 1]

        def put(low, tall, lane, pair):
            smoothed, unsmoothed = (value.astype(jnp.bfloat16) for value in pair)
            wide = unsmoothed.shape[1]
            smooth_y[low : low + tall, lane : lane + wide] = smoothed
            smooth_y[low : low + tall, rows + lane : rows + lane + wide] = smoothed
            plain_y[low : low + tall, lane : lane + wide] = unsmoothed

        tall, wide, edge = 64, min(2 * LANES, rows), 16
        for low in range(0, rows, tall):
            lane = min(max((low - RADIUS - HALO) // LANES, 0) * LANES, rows - wide)
            out_row, in_row = iota((tall, wide), 0) + low, iota((tall, wide), 1) + lane
            put(low, tall, lane, high_pass_inside(out_row, in_row, off_y))
        for low, lane in ((0, 0), (rows - edge, rows - wide)):
            out_row, in_row = iota((edge, wide), 0) + low, iota((edge, wide), 1) + lane
            put(low, edge, lane, high_pass(out_row, in_row, off_y, rows))

        slot = lax.rem(index, PACK)
        source = iota((2 * LANES, LANES), 0)
        target = iota((2 * LANES, LANES), 1)
        side, lane = source // LANES, source % LANES - slot * planes * HALO
        plane, column = lane // HALO, lane % HALO
        chosen = (lane >= 0) & (lane < planes * HALO) & (target == plane * 2 * HALO + side * HALO + column)
        pick = chosen.astype(jnp.float32).astype(jnp.bfloat16)
        edges = dot(jnp.concatenate([left_ref[0], right_ref[0]], axis=1), pick).astype(jnp.bfloat16)

        def across(source):
            column = iota(source.shape, 1)
            second = column >= lanes
            column = jnp.where(second, column - lanes, column)
            gap = source - column + off_x
            low = jnp.where(second | ((column == 0) & (at_start > 0)), 0.0, 1.0)
            high = jnp.where(second | ((column == lanes - 1) & (at_end > 0)), 0.0, 1.0)
            middle = jnp.where(second, 1.0, 2.0)
            return jnp.where(gap == 0, middle, jnp.where(gap == -1, low, jnp.where(gap == 1, high, 0.0)))

        inner = across(iota((lanes, 2 * lanes), 0)).astype(jnp.bfloat16)
        outer = iota((2 * HALO, 2 * lanes), 0)
        outer = across(jnp.where(outer < HALO, outer - HALO, outer - HALO + lanes))

        for pair in range(planes // 2):
            for half in range(2):
                z = 2 * pair + half
                pieces = [outer]
                if z > 0:
                    pieces.insert(0, jnp.zeros((2 * HALO * z, 2 * lanes), jnp.float32))
                left_over = LANES - 2 * HALO * (z + 1)
                pieces.append(jnp.zeros((left_over, 2 * lanes), jnp.float32))
                weights = jnp.concatenate([inner, jnp.concatenate(pieces, axis=0).astype(jnp.bfloat16)], axis=0)
                moved = dot(jnp.concatenate([raw_ref[0, z], edges], axis=1), weights)
                big = moved[:, :lanes].astype(jnp.bfloat16)
                columns = slice(half * lanes, (half + 1) * lanes)
                split[:rows, columns] = big
                split[rows:, columns] = (moved[:, :lanes] - big.astype(jnp.float32)).astype(jnp.bfloat16)
                plain[:, columns] = moved[:, lanes:].astype(jnp.bfloat16)
            smoothed = dot(smooth_y[...], split[...])
            shifted = dot(plain_y[...], plain[...])
            for half in range(2):
                z = 2 * pair + half
                columns = slice(half * lanes, (half + 1) * lanes)
                smooth[HALO + z] = smoothed[:, columns]
                summed[SHIFT + z + off_z] += shifted[:, columns]

        def along(block, carry):
            low = pl.multiple_of(block * strip, strip)
            plane = [smooth[HALO + z - off_z, pl.ds(low, strip), :] for z in range(planes)]
            for z in range(planes):
                value = 2.0 * plane[z]
                if z > 0:
                    value = value + plane[z - 1]
                if z + 1 < planes:
                    value = value + plane[z + 1]
                send_ref[block, 0, z] = (value * (1.0 / (BOX * 64))).astype(jnp.bfloat16)
            return carry

        lax.fori_loop(0, blocks, along, 0)

    if not last:
        frame()

        @pl.when(step == count - 1)
        def _():
            sum_out_ref[...] = summed[SHIFT : SHIFT + planes]
    else:
        pl.when(step < count)(frame)

        @pl.when(step == count)
        def _():
            def hand(block, carry):
                low = pl.multiple_of(block * strip, strip)
                for z in range(planes):
                    send_ref[block, 0, z] = (summed[SHIFT + z, pl.ds(low, strip), :] * (1.0 / BOX)).astype(jnp.bfloat16)
                return carry

            lax.fori_loop(0, blocks, hand, 0)


def register(raw, left, right, meta, summed, first, count, owners, last):
    frames, planes, rows, lanes = raw.shape
    steps = count + 1 if last else count

    edge_spec = pl.BlockSpec((1, rows, LANES), lambda f, m: ((first + jnp.minimum(f, count - 1)) // PACK, 0, 0))
    whole = pl.BlockSpec((planes, rows, lanes), lambda f, m: (0, 0, 0))
    raw_spec = pl.BlockSpec((1, planes, rows, lanes), lambda f, m: (first + jnp.minimum(f, count - 1), 0, 0, 0))
    in_specs = [raw_spec, edge_spec, edge_spec]
    operands = [raw, left, right]
    if first > 0:
        in_specs.append(whole)
        operands.append(summed)
    strip = rows // owners
    out_specs = [pl.BlockSpec((owners, 1, planes, strip, lanes), lambda f, m: (0, f, 0, 0, 0))]
    out_shape = [jax.ShapeDtypeStruct((owners, steps, planes, strip, lanes), jnp.bfloat16)]
    if not last:
        out_specs.append(whole)
        out_shape.append(jax.ShapeDtypeStruct((planes, rows, lanes), jnp.float32))

    def body(*refs):
        register_body(first, count, frames, last, *refs)

    return pl.pallas_call(
        body,
        grid_spec=pltpu.PrefetchScalarGridSpec(
            num_scalar_prefetch=1,
            grid=(steps,),
            in_specs=in_specs,
            out_specs=tuple(out_specs),
            scratch_shapes=[
                pltpu.VMEM((rows, 2 * rows), jnp.bfloat16),
                pltpu.VMEM((rows, rows), jnp.bfloat16),
                pltpu.VMEM((2 * rows, 2 * lanes), jnp.bfloat16),
                pltpu.VMEM((rows, 2 * lanes), jnp.bfloat16),
                pltpu.VMEM((planes + 2 * HALO, rows, lanes), jnp.float32),
                pltpu.VMEM((planes + 2 * SHIFT, rows, lanes), jnp.float32),
            ],
        ),
        out_shape=tuple(out_shape),
        compiler_params=pltpu.CompilerParams(vmem_limit_bytes=VMEM),
        name=f"register_{first}",
    )(meta, *operands)


def spread_body(taps_ref, order_ref, kernel_ref, rowsum_ref):
    total = order_ref.shape[1]
    frame = iota((total, total), 0)
    lag = frame - jnp.broadcast_to(order_ref[0:1, :], (total, total))
    value = jnp.zeros((total, total), jnp.float32)
    for tap in range(TAPS):
        value = jnp.where(lag == tap, taps_ref[tap], value)
    small = value.astype(jnp.bfloat16)
    rowsum = jnp.sum(small.astype(jnp.float32), axis=1, keepdims=True) * (1.0 / total)
    rowsum_ref[...] = jnp.broadcast_to(rowsum[:, :, None], (total, SUB, LANES)).reshape(total * SUB, LANES)
    repeat = iota((total, total * SUB), 1) // SUB == iota((total, total * SUB), 0)
    wide = dot(small, repeat.astype(jnp.float32).astype(jnp.bfloat16))
    tall = jnp.broadcast_to(wide[:, None, :], (total, SUB, total * SUB)).reshape(total * SUB, total * SUB)
    same = iota(tall.shape, 0) % SUB == iota(tall.shape, 1) % SUB
    kernel_ref[...] = jnp.where(same, tall, 0.0).astype(jnp.bfloat16)


def spread_kernel(taps, order):
    total = order.shape[1]
    return pl.pallas_call(
        spread_body,
        in_specs=[pl.BlockSpec(memory_space=pltpu.SMEM), pl.BlockSpec(memory_space=pltpu.VMEM)],
        out_shape=(
            jax.ShapeDtypeStruct((total * SUB, total * SUB), jnp.bfloat16),
            jax.ShapeDtypeStruct((total * SUB, LANES), jnp.float32),
        ),
        compiler_params=pltpu.CompilerParams(vmem_limit_bytes=VMEM),
        name="spread_kernel",
    )(taps, order)


def filter_body(group, kernel_ref, rowsum_ref, *refs):
    *got, out_ref, template_ref = refs
    owners = got[0].shape[0]
    total, _, strip, lanes = out_ref.shape
    frames = group * (total // owners)
    width = frames * SUB
    reach = -(-TAPS // frames)

    sent = got[-1][:, CHUNKS[-1], 0].astype(jnp.float32)
    template_ref[0] = jnp.sum(sent, axis=0) * (1.0 / total)

    for pair in range(strip // (2 * SUB)):
        tiles = []
        for j in range(owners // group):
            halves = []
            for half in range(2):
                low = (2 * pair + half) * SUB
                parts = []
                for ref, count in zip(got, CHUNKS):
                    part = ref[group * j : group * (j + 1), 0:count, 0, low : low + SUB, :]
                    parts.append(part.reshape(group * count * SUB, lanes))
                halves.append(jnp.concatenate(parts, axis=0))
            tiles.append(jnp.concatenate(halves, axis=1))
        mean = sum(jnp.sum(t.astype(jnp.float32).reshape(frames, SUB, 2 * lanes), axis=0) for t in tiles)
        for i in range(len(tiles)):
            lowest = max(0, i - reach)
            rows = slice(i * width, (i + 1) * width)
            value = None
            for j in range(lowest, i + 1):
                part = dot(kernel_ref[rows, j * width : (j + 1) * width], tiles[j])
                value = part if value is None else value + part
            rowsum = rowsum_ref[rows, :].reshape(frames, SUB, lanes)
            value = value.reshape(frames, SUB, 2 * lanes)
            done = [
                value[:, :, h * lanes : (h + 1) * lanes] - rowsum * mean[None, :, h * lanes : (h + 1) * lanes]
                for h in range(2)
            ]
            both = jnp.concatenate(done, axis=1).astype(jnp.bfloat16)
            out_ref[i * frames : (i + 1) * frames, 0, 2 * SUB * pair : 2 * SUB * (pair + 1), :] = both


def filter_frames(kernel, rowsum, got, total, group):
    owners, _, planes, strip, lanes = got[0].shape
    in_specs = [
        pl.BlockSpec(kernel.shape, lambda z: (0, 0)),
        pl.BlockSpec(rowsum.shape, lambda z: (0, 0)),
    ]
    for part in got:
        in_specs.append(pl.BlockSpec((owners, part.shape[1], 1, strip, lanes), lambda z: (0, 0, z, 0, 0)))

    def body(*refs):
        filter_body(group, *refs)

    return pl.pallas_call(
        body,
        grid=(planes,),
        in_specs=in_specs,
        out_specs=(
            pl.BlockSpec((total, 1, strip, lanes), lambda z: (0, z, 0, 0)),
            pl.BlockSpec((1, strip, lanes), lambda z: (z, 0, 0)),
        ),
        out_shape=(
            jax.ShapeDtypeStruct((total, planes, strip, lanes), jnp.bfloat16),
            jax.ShapeDtypeStruct((planes, strip, lanes), jnp.float32),
        ),
        compiler_params=pltpu.CompilerParams(vmem_limit_bytes=VMEM),
        name="filter_frames",
    )(kernel, rowsum, *got)


def local(raw, offsets, taps):
    frame_dev, planes, rows, lanes = raw.shape
    owners = lax.axis_size("frames")
    tiles = lax.axis_size("tiles")
    total = frame_dev * owners
    group = min(owners, 4)

    first_columns, last_columns = pack_edges(raw)
    upward = [(i, i + 1) for i in range(tiles - 1)]
    left = lax.ppermute(last_columns, "tiles", upward)
    right = lax.ppermute(first_columns, "tiles", [(j, i) for i, j in upward])

    tile = lax.axis_index("tiles")
    ends = jnp.stack([tile == 0, tile == tiles - 1]).astype(jnp.int32)
    meta = jnp.concatenate([offsets.reshape(-1), ends])

    order = []
    for block in range(owners // group):
        low = 0
        for count in CHUNKS:
            for owner in range(group * block, group * (block + 1)):
                order += [owner * frame_dev + low + f for f in range(count)]
            low += count
    kernel, rowsum = spread_kernel(taps, jnp.tile(jnp.array(order, jnp.int32)[None], (SUB, 1)))

    got = []
    summed = None
    low = 0
    for number, count in enumerate(CHUNKS):
        is_last = number == len(CHUNKS) - 1
        made = register(raw, left, right, meta, summed, low, count, owners, is_last)
        if not is_last:
            summed = made[1]
        got.append(lax.all_to_all(made[0], "frames", split_axis=0, concat_axis=0, tiled=True))
        low += count
    return filter_frames(kernel, rowsum, got, total, group)


def solution(mesh):
    placed = (P("frames", None, None, "tiles"), P("frames", None), P())
    return jax.shard_map(
        local,
        mesh=mesh,
        in_specs=placed,
        out_specs=(P(None, None, "frames", "tiles"), P(None, "frames", "tiles")),
        check_vma=False,
    )
```

```python
import jax
import jax.numpy as jnp
from jax import lax
from jax.experimental import pallas as pl
from jax.experimental.pallas import tpu as pltpu
from jax.sharding import PartitionSpec as P


TAPS = 64
SHIFT = 3
RADIUS = 8
HALO = SHIFT + 1
BOX = 2 * RADIUS + 1
LANES = 128
SUB = 8
CHUNKS = (2, 6)
PACK = 2
VMEM = 56 << 20


def iota(shape, dim):
    return lax.broadcasted_iota(jnp.int32, shape, dim)


def dot(a, b):
    return jnp.dot(a, b, preferred_element_type=jnp.float32)


def pack_body(*refs):
    *raw_refs, first_ref, last_ref, pick = refs
    planes, rows, lanes = raw_refs[0].shape[1:]
    half_rows = rows // 2
    half_lanes = PACK * planes * HALO

    @pl.when(pl.program_id(0) == 0)
    def _():
        pick[...] = jnp.zeros(pick.shape, pick.dtype)
        low, lane = iota((SUB, LANES), 0), iota((SUB, LANES), 1)
        for half in range(2):
            for f in range(PACK):
                for z in range(planes):
                    start = half * half_lanes + (f * planes + z) * HALO
                    head = (low < HALO) & (lane == start + low)
                    tail = (low >= SUB - HALO) & (lane == start + low - (SUB - HALO))
                    row = (f * planes + z) * lanes
                    pick[half, row : row + SUB, :LANES] = head.astype(jnp.float32).astype(jnp.bfloat16)
                    row += lanes - SUB
                    pick[half, row : row + SUB, LANES:] = tail.astype(jnp.float32).astype(jnp.bfloat16)

    edges = 0.0
    for half in range(2):
        part = slice(half * half_rows, (half + 1) * half_rows)
        wide = [raw_ref[0, z, part] for raw_ref in raw_refs for z in range(planes)]
        edges = edges + dot(jnp.concatenate(wide, axis=1), pick[half])
    edges = edges.astype(jnp.bfloat16)
    first_ref[0] = edges[:, :LANES]
    last_ref[0] = edges[:, LANES:]


def pack_edges(raw, first, count):
    _, planes, rows, lanes = raw.shape
    edge = jax.ShapeDtypeStruct((count // PACK, rows // 2, LANES), jnp.bfloat16)
    spec = pl.BlockSpec((1, rows // 2, LANES), lambda i: (i, 0, 0))
    return pl.pallas_call(
        pack_body,
        grid=(count // PACK,),
        in_specs=[
            pl.BlockSpec((1, planes, rows, lanes), lambda i, f=f: (first + i * PACK + f, 0, 0, 0)) for f in range(PACK)
        ],
        out_specs=(spec, spec),
        out_shape=(edge, edge),
        scratch_shapes=[pltpu.VMEM((2, PACK * planes * lanes, 2 * LANES), jnp.bfloat16)],
        compiler_params=pltpu.CompilerParams(vmem_limit_bytes=VMEM),
    )(*[raw] * PACK)


def high_pass(out_row, in_row, off_y, rows):
    smoothed = 0.0
    for delta, weight in ((-1, 1.0), (1, 1.0), (0, 2.0)):
        reached = out_row + delta
        source = reached - off_y
        inside = (reached >= 0) & (reached < rows) & (source >= 0) & (source < rows)
        gap = jnp.abs(in_row - source)
        term = jnp.where(gap == 0, BOX - 1.0, jnp.where(gap <= RADIUS, -1.0, 0.0))
        term = jnp.where(inside, term, 0.0)
        smoothed = smoothed + weight * term
    return smoothed, term


def high_pass_inside(out_row, in_row, off_y):
    gap = jnp.abs(in_row - out_row + off_y)
    plain = jnp.where(gap == 0, BOX - 1.0, jnp.where(gap <= RADIUS, -1.0, 0.0))
    far = jnp.where(gap <= RADIUS - 1, -4.0, jnp.where(gap == RADIUS, -3.0, jnp.where(gap == RADIUS + 1, -1.0, 0.0)))
    smoothed = jnp.where(gap == 0, 2.0 * BOX - 4.0, jnp.where(gap == 1, BOX - 4.0, far))
    return smoothed, plain


def register_body(first, count, total, last, meta_ref, raw_ref, left_ref, right_ref, *rest):
    if first > 0:
        sum_in_ref, *rest = rest
    send_ref, *rest = rest
    if not last:
        sum_out_ref, *rest = rest
    smooth_y, plain_y, split, plain, smooth, summed = rest
    planes, rows, lanes = raw_ref.shape[1:]
    blocks = send_ref.shape[0]
    strip = rows // blocks
    step = pl.program_id(0)

    @pl.when(step == 0)
    def _():
        smooth_y[...] = jnp.zeros(smooth_y.shape, smooth_y.dtype)
        plain_y[...] = jnp.zeros(plain_y.shape, plain_y.dtype)
        smooth[0:HALO] = jnp.zeros((HALO, rows, lanes), jnp.float32)
        smooth[HALO + planes :] = jnp.zeros((HALO, rows, lanes), jnp.float32)
        if first > 0:
            summed[SHIFT : SHIFT + planes] = sum_in_ref[...]
        else:
            summed[SHIFT : SHIFT + planes] = jnp.zeros((planes, rows, lanes), jnp.float32)

    def frame():
        index = first + step
        off_z, off_y, off_x = meta_ref[3 * index], meta_ref[3 * index + 1], meta_ref[3 * index + 2]
        at_start, at_end = meta_ref[3 * total], meta_ref[3 * total + 1]

        def put(low, tall, lane, pair):
            smoothed, unsmoothed = (value.astype(jnp.bfloat16) for value in pair)
            wide = unsmoothed.shape[1]
            smooth_y[low : low + tall, lane : lane + wide] = smoothed
            smooth_y[low : low + tall, rows + lane : rows + lane + wide] = smoothed
            plain_y[low : low + tall, lane : lane + wide] = unsmoothed

        tall, wide, edge = 64, min(2 * LANES, rows), 16
        for low in range(0, rows, tall):
            lane = min(max((low - RADIUS - HALO) // LANES, 0) * LANES, rows - wide)
            out_row, in_row = iota((tall, wide), 0) + low, iota((tall, wide), 1) + lane
            put(low, tall, lane, high_pass_inside(out_row, in_row, off_y))
        for low, lane in ((0, 0), (rows - edge, rows - wide)):
            out_row, in_row = iota((edge, wide), 0) + low, iota((edge, wide), 1) + lane
            put(low, edge, lane, high_pass(out_row, in_row, off_y, rows))

        slot = lax.rem(step, PACK)
        source = iota((2 * LANES, LANES), 0)
        target = iota((2 * LANES, LANES), 1)
        side, lane = source // LANES, source % LANES - slot * planes * HALO
        packed = jnp.concatenate([left_ref[0], right_ref[0]], axis=1)
        edges = []
        for half in range(2):
            own = lane - half * PACK * planes * HALO
            plane, column = own // HALO, own % HALO
            chosen = (own >= 0) & (own < planes * HALO) & (target == plane * 2 * HALO + side * HALO + column)
            edges.append(dot(packed, chosen.astype(jnp.float32).astype(jnp.bfloat16)).astype(jnp.bfloat16))
        edges = jnp.concatenate(edges, axis=0)

        def across(source):
            column = iota(source.shape, 1)
            second = column >= lanes
            column = jnp.where(second, column - lanes, column)
            gap = source - column + off_x
            low = jnp.where(second | ((column == 0) & (at_start > 0)), 0.0, 1.0)
            high = jnp.where(second | ((column == lanes - 1) & (at_end > 0)), 0.0, 1.0)
            middle = jnp.where(second, 1.0, 2.0)
            return jnp.where(gap == 0, middle, jnp.where(gap == -1, low, jnp.where(gap == 1, high, 0.0)))

        inner = across(iota((lanes, 2 * lanes), 0)).astype(jnp.bfloat16)
        outer = iota((2 * HALO, 2 * lanes), 0)
        outer = across(jnp.where(outer < HALO, outer - HALO, outer - HALO + lanes))

        for pair in range(planes // 2):
            for half in range(2):
                z = 2 * pair + half
                pieces = [outer]
                if z > 0:
                    pieces.insert(0, jnp.zeros((2 * HALO * z, 2 * lanes), jnp.float32))
                left_over = LANES - 2 * HALO * (z + 1)
                pieces.append(jnp.zeros((left_over, 2 * lanes), jnp.float32))
                weights = jnp.concatenate([inner, jnp.concatenate(pieces, axis=0).astype(jnp.bfloat16)], axis=0)
                moved = dot(jnp.concatenate([raw_ref[0, z], edges], axis=1), weights)
                big = moved[:, :lanes].astype(jnp.bfloat16)
                columns = slice(half * lanes, (half + 1) * lanes)
                split[:rows, columns] = big
                split[rows:, columns] = (moved[:, :lanes] - big.astype(jnp.float32)).astype(jnp.bfloat16)
                plain[:, columns] = moved[:, lanes:].astype(jnp.bfloat16)
            smoothed = dot(smooth_y[...], split[...])
            shifted = dot(plain_y[...], plain[...])
            for half in range(2):
                z = 2 * pair + half
                columns = slice(half * lanes, (half + 1) * lanes)
                smooth[HALO + z] = smoothed[:, columns]
                summed[SHIFT + z + off_z] += shifted[:, columns]

        def along(block, carry):
            low = pl.multiple_of(block * strip, strip)
            plane = [smooth[HALO + z - off_z, pl.ds(low, strip), :] for z in range(planes)]
            for z in range(planes):
                value = 2.0 * plane[z]
                if z > 0:
                    value = value + plane[z - 1]
                if z + 1 < planes:
                    value = value + plane[z + 1]
                send_ref[block, 0, z] = (value * (1.0 / (BOX * 64))).astype(jnp.bfloat16)
            return carry

        lax.fori_loop(0, blocks, along, 0)

    if not last:
        frame()

        @pl.when(step == count - 1)
        def _():
            sum_out_ref[...] = summed[SHIFT : SHIFT + planes]
    else:
        pl.when(step < count)(frame)

        @pl.when(step == count)
        def _():
            def hand(block, carry):
                low = pl.multiple_of(block * strip, strip)
                for z in range(planes):
                    send_ref[block, 0, z] = (summed[SHIFT + z, pl.ds(low, strip), :] * (1.0 / BOX)).astype(jnp.bfloat16)
                return carry

            lax.fori_loop(0, blocks, hand, 0)


def register(raw, left, right, meta, summed, first, count, owners, last):
    frames, planes, rows, lanes = raw.shape
    steps = count + 1 if last else count

    edge_spec = pl.BlockSpec((1, rows // 2, LANES), lambda f, m: (jnp.minimum(f, count - 1) // PACK, 0, 0))
    whole = pl.BlockSpec((planes, rows, lanes), lambda f, m: (0, 0, 0))
    raw_spec = pl.BlockSpec((1, planes, rows, lanes), lambda f, m: (first + jnp.minimum(f, count - 1), 0, 0, 0))
    in_specs = [raw_spec, edge_spec, edge_spec]
    operands = [raw, left, right]
    if first > 0:
        in_specs.append(whole)
        operands.append(summed)
    strip = rows // owners
    out_specs = [pl.BlockSpec((owners, 1, planes, strip, lanes), lambda f, m: (0, f, 0, 0, 0))]
    out_shape = [jax.ShapeDtypeStruct((owners, steps, planes, strip, lanes), jnp.bfloat16)]
    if not last:
        out_specs.append(whole)
        out_shape.append(jax.ShapeDtypeStruct((planes, rows, lanes), jnp.float32))

    def body(*refs):
        register_body(first, count, frames, last, *refs)

    return pl.pallas_call(
        body,
        grid_spec=pltpu.PrefetchScalarGridSpec(
            num_scalar_prefetch=1,
            grid=(steps,),
            in_specs=in_specs,
            out_specs=tuple(out_specs),
            scratch_shapes=[
                pltpu.VMEM((rows, 2 * rows), jnp.bfloat16),
                pltpu.VMEM((rows, rows), jnp.bfloat16),
                pltpu.VMEM((2 * rows, 2 * lanes), jnp.bfloat16),
                pltpu.VMEM((rows, 2 * lanes), jnp.bfloat16),
                pltpu.VMEM((planes + 2 * HALO, rows, lanes), jnp.float32),
                pltpu.VMEM((planes + 2 * SHIFT, rows, lanes), jnp.float32),
            ],
        ),
        out_shape=tuple(out_shape),
        compiler_params=pltpu.CompilerParams(vmem_limit_bytes=VMEM),
    )(meta, *operands)


def spread_body(taps_ref, order_ref, kernel_ref, rowsum_ref):
    total = rowsum_ref.shape[0] // SUB
    frames = order_ref.shape[1] // 2
    reach = kernel_ref.shape[1] // (frames * SUB) - 1
    for back in range(reach + 1):
        lag = iota((frames, 2 * frames), 0) + (back * frames - order_ref[0:1, :])
        value = jnp.zeros(lag.shape, jnp.float32)
        for tap in range(TAPS):
            value = jnp.where(lag == tap, taps_ref[tap], value)
        small = value.astype(jnp.bfloat16)
        shape = (2 * frames, frames * SUB)
        repeat = iota(shape, 1) // SUB == iota(shape, 0)
        wide = dot(small, repeat.astype(jnp.float32).astype(jnp.bfloat16))
        width = frames * SUB
        tall = jnp.broadcast_to(wide[:, None, :], (frames, SUB, width)).reshape(width, width)
        same = iota(tall.shape, 0) % SUB == iota(tall.shape, 1) % SUB
        low = (reach - back) * width
        kernel_ref[:, low : low + width] = jnp.where(same, tall, 0.0).astype(jnp.bfloat16)

    lag = iota((total, LANES), 0) - iota((total, LANES), 1)
    value = jnp.zeros(lag.shape, jnp.float32)
    for tap in range(TAPS):
        value = jnp.where((lag >= 0) & (iota(lag.shape, 1) == tap), taps_ref[tap], value)
    rowsum = jnp.sum(value.astype(jnp.bfloat16).astype(jnp.float32), axis=1, keepdims=True) * (1.0 / total)
    rowsum_ref[...] = jnp.broadcast_to(rowsum[:, :, None], (total, SUB, LANES)).reshape(total * SUB, LANES)


def spread_kernel(taps, order, total, frames, reach):
    def body(*refs):
        spread_body(*refs)

    return pl.pallas_call(
        body,
        in_specs=[pl.BlockSpec(memory_space=pltpu.SMEM), pl.BlockSpec(memory_space=pltpu.VMEM)],
        out_shape=(
            jax.ShapeDtypeStruct((frames * SUB, (reach + 1) * frames * SUB), jnp.bfloat16),
            jax.ShapeDtypeStruct((total * SUB, LANES), jnp.float32),
        ),
        compiler_params=pltpu.CompilerParams(vmem_limit_bytes=VMEM),
        name="spread_kernel",
    )(taps, order)


def filter_body(groups, kernel_ref, rowsum_ref, *refs):
    *got, out_ref, template_ref, done, sems = refs
    group = got[0].shape[0]
    strip, lanes = done.shape[2:]
    total = done.shape[1]
    frames = total // groups
    width = frames * SUB
    reach = kernel_ref.shape[1] // width - 1
    step = pl.program_id(0)
    slot = lax.rem(step, 2)
    got = [got[c * groups : (c + 1) * groups] for c in range(len(CHUNKS))]

    def copy(z, slot, i):
        part = pl.ds(i * frames, frames)
        return pltpu.make_async_copy(done.at[slot, part], out_ref.at[part, z], sems.at[slot, i])

    sent = sum(jnp.sum(ref[:, CHUNKS[-1], 0].astype(jnp.float32), axis=0) for ref in got[-1])
    template_ref[0] = sent * (1.0 / total)

    tiles = []
    means = []
    for pair in range(strip // (2 * SUB)):
        stack = []
        for j in range(groups):
            halves = []
            for half in range(2):
                low = (2 * pair + half) * SUB
                parts = []
                for refs, count in zip(got, CHUNKS):
                    part = refs[j][:, 0:count, 0, low : low + SUB, :]
                    parts.append(part.reshape(group * count * SUB, lanes))
                halves.append(jnp.concatenate(parts, axis=0))
            stack.append(jnp.concatenate(halves, axis=1))
        means.append(sum(jnp.sum(t.astype(jnp.float32).reshape(frames, SUB, 2 * lanes), axis=0) for t in stack))
        tiles.append(stack)

    @pl.when(step >= 2)
    def _():
        for i in range(groups):
            copy(step - 2, slot, i).wait()

    for i in range(groups):
        rows = slice(i * width, (i + 1) * width)
        for pair in range(len(tiles)):
            lowest = max(0, i - reach)
            value = dot(
                kernel_ref[:, (reach - i + lowest) * width :],
                jnp.concatenate(tiles[pair][lowest : i + 1], axis=0),
            ).reshape(frames, SUB, 2 * lanes)
            rowsum = rowsum_ref[rows, :].reshape(frames, SUB, lanes)
            both = [
                value[:, :, h * lanes : (h + 1) * lanes] - rowsum * means[pair][None, :, h * lanes : (h + 1) * lanes]
                for h in range(2)
            ]
            both = jnp.concatenate(both, axis=1).astype(jnp.bfloat16)
            done[slot, i * frames : (i + 1) * frames, 2 * SUB * pair : 2 * SUB * (pair + 1), :] = both
        copy(step, slot, i).start()

    @pl.when(step == pl.num_programs(0) - 1)
    def _():
        for i in range(groups):
            copy(step - 1, 1 - slot, i).wait()
        for i in range(groups):
            copy(step, slot, i).wait()


def filter_frames(kernel, rowsum, got, total, group):
    owners, _, planes, strip, lanes = got[0].shape
    groups = owners // group
    in_specs = [
        pl.BlockSpec(kernel.shape, lambda z: (0, 0)),
        pl.BlockSpec(rowsum.shape, lambda z: (0, 0)),
    ]
    operands = []
    for part in got:
        for j in range(groups):
            in_specs.append(pl.BlockSpec((group, part.shape[1], 1, strip, lanes), lambda z, j=j: (j, 0, z, 0, 0)))
            operands.append(part)

    def body(*refs):
        filter_body(groups, *refs)

    return pl.pallas_call(
        body,
        grid=(planes,),
        in_specs=in_specs,
        out_specs=(
            pl.BlockSpec(memory_space=pl.ANY),
            pl.BlockSpec((1, strip, lanes), lambda z: (z, 0, 0)),
        ),
        out_shape=(
            jax.ShapeDtypeStruct((total, planes, strip, lanes), jnp.bfloat16),
            jax.ShapeDtypeStruct((planes, strip, lanes), jnp.float32),
        ),
        scratch_shapes=[pltpu.VMEM((2, total, strip, lanes), jnp.bfloat16), pltpu.SemaphoreType.DMA((2, groups))],
        compiler_params=pltpu.CompilerParams(vmem_limit_bytes=VMEM),
        name="filter_frames",
    )(kernel, rowsum, *operands)


def local(raw, offsets, taps):
    frame_dev, _, _, _ = raw.shape
    owners = lax.axis_size("frames")
    tiles = lax.axis_size("tiles")
    total = frame_dev * owners
    group = min(owners, 4)

    upward = [(i, i + 1) for i in range(tiles - 1)]
    sides = []
    low = 0
    for count in CHUNKS:
        first_columns, last_columns = pack_edges(raw, low, count)
        left = lax.ppermute(last_columns, "tiles", upward)
        right = lax.ppermute(first_columns, "tiles", [(j, i) for i, j in upward])
        sides.append((left, right))
        low += count

    tile = lax.axis_index("tiles")
    ends = jnp.stack([tile == 0, tile == tiles - 1]).astype(jnp.int32)
    meta = jnp.concatenate([offsets.reshape(-1), ends])

    order = []
    low = 0
    for count in CHUNKS:
        for owner in range(group):
            order += [owner * frame_dev + low + f for f in range(count)]
        low += count
    frames = group * frame_dev
    reach = min(-(-TAPS // frames), owners // group - 1)
    order = jnp.array(order + [1 << 20] * frames, jnp.int32)
    kernel, rowsum = spread_kernel(taps, jnp.tile(order[None], (SUB, 1)), total, frames, reach)

    got = []
    summed = None
    low = 0
    for number, count in enumerate(CHUNKS):
        is_last = number == len(CHUNKS) - 1
        made = register(raw, *sides[number], meta, summed, low, count, owners, is_last)
        if not is_last:
            summed = made[1]
        got.append(lax.all_to_all(made[0], "frames", split_axis=0, concat_axis=0, tiled=True))
        low += count
    return filter_frames(kernel, rowsum, got, total, group)


def solution(mesh):
    placed = (P("frames", None, None, "tiles"), P("frames", None), P())
    return jax.shard_map(
        local,
        mesh=mesh,
        in_specs=placed,
        out_specs=(P(None, None, "frames", "tiles"), P(None, "frames", "tiles")),
        check_vma=False,
    )
```

```python
import jax
import jax.numpy as jnp
from jax import lax
from jax.experimental import pallas as pl
from jax.experimental.pallas import tpu as pltpu
from jax.sharding import PartitionSpec as P


TAPS = 64
SHIFT = 3
RADIUS = 8
HALO = SHIFT + 1
BOX = 2 * RADIUS + 1
LANES = 128
SUB = 8
CHUNKS = (2, 6)
PACK = LANES // (8 * HALO)
VMEM = 56 << 20


def iota(shape, dim):
    return lax.broadcasted_iota(jnp.int32, shape, dim)


def dot(a, b):
    return jnp.dot(a, b, preferred_element_type=jnp.float32)


def pack_body(*refs):
    *raw_refs, first_ref, last_ref, pick = refs
    step = pl.program_id(0)
    planes, _, lanes = raw_refs[0].shape[1:]
    half = lax.rem(step, PACK // len(raw_refs))

    @pl.when(step == 0)
    def _():
        pick[...] = jnp.zeros(pick.shape, pick.dtype)

    low, lane = iota((SUB, LANES), 0), iota((SUB, LANES), 1)
    wide = []
    for f, raw_ref in enumerate(raw_refs):
        for z in range(planes):
            start = ((half * len(raw_refs) + f) * planes + z) * HALO
            head = (low < HALO) & (lane == start + low)
            tail = (low >= SUB - HALO) & (lane == start + low - (SUB - HALO))
            row = (f * planes + z) * lanes
            pick[row : row + SUB, :LANES] = head.astype(jnp.float32).astype(jnp.bfloat16)
            pick[row + lanes - SUB : row + lanes, LANES:] = tail.astype(jnp.float32).astype(jnp.bfloat16)
            wide.append(raw_ref[0, z])
    edges = dot(jnp.concatenate(wide, axis=1), pick[...]).astype(jnp.bfloat16)

    @pl.when(half == 0)
    def _():
        first_ref[0] = edges[:, :LANES]
        last_ref[0] = edges[:, LANES:]

    @pl.when(half != 0)
    def _():
        first_ref[0] += edges[:, :LANES]
        last_ref[0] += edges[:, LANES:]


def pack_edges(raw):
    frames, planes, rows, lanes = raw.shape
    each = 2
    edge = jax.ShapeDtypeStruct((frames // PACK, rows, LANES), jnp.bfloat16)
    spec = pl.BlockSpec((1, rows, LANES), lambda i: (i * each // PACK, 0, 0))
    return pl.pallas_call(
        pack_body,
        grid=(frames // each,),
        in_specs=[
            pl.BlockSpec((1, planes, rows, lanes), lambda i, f=f: (i * each + f, 0, 0, 0)) for f in range(each)
        ],
        out_specs=(spec, spec),
        out_shape=(edge, edge),
        scratch_shapes=[pltpu.VMEM((each * planes * lanes, 2 * LANES), jnp.bfloat16)],
        compiler_params=pltpu.CompilerParams(vmem_limit_bytes=VMEM),
        name="pack_edges",
    )(*[raw] * each)


def high_pass(out_row, in_row, off_y, rows):
    smoothed = 0.0
    for delta, weight in ((-1, 1.0), (1, 1.0), (0, 2.0)):
        reached = out_row + delta
        source = reached - off_y
        inside = (reached >= 0) & (reached < rows) & (source >= 0) & (source < rows)
        gap = jnp.abs(in_row - source)
        term = jnp.where(gap == 0, BOX - 1.0, jnp.where(gap <= RADIUS, -1.0, 0.0))
        term = jnp.where(inside, term, 0.0)
        smoothed = smoothed + weight * term
    return smoothed, term


def high_pass_inside(out_row, in_row, off_y):
    gap = jnp.abs(in_row - out_row + off_y)
    plain = jnp.where(gap == 0, BOX - 1.0, jnp.where(gap <= RADIUS, -1.0, 0.0))
    far = jnp.where(gap <= RADIUS - 1, -4.0, jnp.where(gap == RADIUS, -3.0, jnp.where(gap == RADIUS + 1, -1.0, 0.0)))
    smoothed = jnp.where(gap == 0, 2.0 * BOX - 4.0, jnp.where(gap == 1, BOX - 4.0, far))
    return smoothed, plain


def register_body(first, count, total, meta_ref, raw_ref, left_ref, right_ref, *rest):
    if first > 0:
        sum_in_ref, *rest = rest
    send_ref, sum_out_ref, *rest = rest
    smooth_y, plain_y, split, plain, smooth, summed = rest
    planes, rows, lanes = raw_ref.shape[1:]
    blocks = send_ref.shape[0]
    strip = rows // blocks
    step = pl.program_id(0)

    @pl.when(step == 0)
    def _():
        smooth_y[...] = jnp.zeros(smooth_y.shape, smooth_y.dtype)
        plain_y[...] = jnp.zeros(plain_y.shape, plain_y.dtype)
        smooth[0:HALO] = jnp.zeros((HALO, rows, lanes), jnp.float32)
        smooth[HALO + planes :] = jnp.zeros((HALO, rows, lanes), jnp.float32)
        if first > 0:
            summed[SHIFT : SHIFT + planes] = sum_in_ref[...] * BOX
        else:
            summed[SHIFT : SHIFT + planes] = jnp.zeros((planes, rows, lanes), jnp.float32)

    def frame():
        index = first + step
        off_z, off_y, off_x = meta_ref[3 * index], meta_ref[3 * index + 1], meta_ref[3 * index + 2]
        at_start, at_end = meta_ref[3 * total], meta_ref[3 * total + 1]

        def put(low, tall, lane, pair):
            smoothed, unsmoothed = (value.astype(jnp.bfloat16) for value in pair)
            wide = unsmoothed.shape[1]
            smooth_y[low : low + tall, lane : lane + wide] = smoothed
            smooth_y[low : low + tall, rows + lane : rows + lane + wide] = smoothed
            plain_y[low : low + tall, lane : lane + wide] = unsmoothed

        tall, wide, edge = 64, min(2 * LANES, rows), 16
        for low in range(0, rows, tall):
            lane = min(max((low - RADIUS - HALO) // LANES, 0) * LANES, rows - wide)
            out_row, in_row = iota((tall, wide), 0) + low, iota((tall, wide), 1) + lane
            put(low, tall, lane, high_pass_inside(out_row, in_row, off_y))
        for low, lane in ((0, 0), (rows - edge, rows - wide)):
            out_row, in_row = iota((edge, wide), 0) + low, iota((edge, wide), 1) + lane
            put(low, edge, lane, high_pass(out_row, in_row, off_y, rows))

        slot = lax.rem(index, PACK)
        source = iota((2 * LANES, LANES), 0)
        target = iota((2 * LANES, LANES), 1)
        side, lane = source // LANES, source % LANES - slot * planes * HALO
        plane, column = lane // HALO, lane % HALO
        chosen = (lane >= 0) & (lane < planes * HALO) & (target == plane * 2 * HALO + side * HALO + column)
        pick = chosen.astype(jnp.float32).astype(jnp.bfloat16)
        edges = dot(jnp.concatenate([left_ref[0], right_ref[0]], axis=1), pick).astype(jnp.bfloat16)

        def across(source):
            column = iota(source.shape, 1)
            second = column >= lanes
            column = jnp.where(second, column - lanes, column)
            gap = source - column + off_x
            low = jnp.where(second | ((column == 0) & (at_start > 0)), 0.0, 1.0)
            high = jnp.where(second | ((column == lanes - 1) & (at_end > 0)), 0.0, 1.0)
            middle = jnp.where(second, 1.0, 2.0)
            return jnp.where(gap == 0, middle, jnp.where(gap == -1, low, jnp.where(gap == 1, high, 0.0)))

        inner = across(iota((lanes, 2 * lanes), 0)).astype(jnp.bfloat16)
        outer = iota((2 * HALO, 2 * lanes), 0)
        outer = across(jnp.where(outer < HALO, outer - HALO, outer - HALO + lanes))

        for pair in range(planes // 2):
            for half in range(2):
                z = 2 * pair + half
                pieces = [outer]
                if z > 0:
                    pieces.insert(0, jnp.zeros((2 * HALO * z, 2 * lanes), jnp.float32))
                left_over = LANES - 2 * HALO * (z + 1)
                pieces.append(jnp.zeros((left_over, 2 * lanes), jnp.float32))
                weights = jnp.concatenate([inner, jnp.concatenate(pieces, axis=0).astype(jnp.bfloat16)], axis=0)
                moved = dot(jnp.concatenate([raw_ref[0, z], edges], axis=1), weights)
                big = moved[:, :lanes].astype(jnp.bfloat16)
                columns = slice(half * lanes, (half + 1) * lanes)
                split[:rows, columns] = big
                split[rows:, columns] = (moved[:, :lanes] - big.astype(jnp.float32)).astype(jnp.bfloat16)
                plain[:, columns] = moved[:, lanes:].astype(jnp.bfloat16)
            smoothed = dot(smooth_y[...], split[...])
            shifted = dot(plain_y[...], plain[...])
            for half in range(2):
                z = 2 * pair + half
                columns = slice(half * lanes, (half + 1) * lanes)
                smooth[HALO + z] = smoothed[:, columns]
                summed[SHIFT + z + off_z] += shifted[:, columns]

        def along(block, carry):
            low = pl.multiple_of(block * strip, strip)
            plane = [smooth[HALO + z - off_z, pl.ds(low, strip), :] for z in range(planes)]
            for z in range(planes):
                value = 2.0 * plane[z]
                if z > 0:
                    value = value + plane[z - 1]
                if z + 1 < planes:
                    value = value + plane[z + 1]
                send_ref[block, 0, z] = (value * (1.0 / (BOX * 64))).astype(jnp.bfloat16)
            return carry

        lax.fori_loop(0, blocks, along, 0)

    frame()

    @pl.when(step == count - 1)
    def _():
        sum_out_ref[...] = summed[SHIFT : SHIFT + planes] * (1.0 / BOX)


def register(raw, left, right, meta, summed, first, count, owners):
    frames, planes, rows, lanes = raw.shape

    edge_spec = pl.BlockSpec((1, rows, LANES), lambda f, m: ((first + f) // PACK, 0, 0))
    whole = pl.BlockSpec((planes, rows, lanes), lambda f, m: (0, 0, 0))
    raw_spec = pl.BlockSpec((1, planes, rows, lanes), lambda f, m: (first + f, 0, 0, 0))
    in_specs = [raw_spec, edge_spec, edge_spec]
    operands = [raw, left, right]
    if first > 0:
        in_specs.append(whole)
        operands.append(summed)
    strip = rows // owners
    out_specs = [pl.BlockSpec((owners, 1, planes, strip, lanes), lambda f, m: (0, f, 0, 0, 0))]
    out_shape = [jax.ShapeDtypeStruct((owners, count, planes, strip, lanes), jnp.bfloat16)]
    out_specs.append(whole)
    out_shape.append(jax.ShapeDtypeStruct((planes, rows, lanes), jnp.float32))

    def body(*refs):
        register_body(first, count, frames, *refs)

    return pl.pallas_call(
        body,
        grid_spec=pltpu.PrefetchScalarGridSpec(
            num_scalar_prefetch=1,
            grid=(count,),
            in_specs=in_specs,
            out_specs=tuple(out_specs),
            scratch_shapes=[
                pltpu.VMEM((rows, 2 * rows), jnp.bfloat16),
                pltpu.VMEM((rows, rows), jnp.bfloat16),
                pltpu.VMEM((2 * rows, 2 * lanes), jnp.bfloat16),
                pltpu.VMEM((rows, 2 * lanes), jnp.bfloat16),
                pltpu.VMEM((planes + 2 * HALO, rows, lanes), jnp.float32),
                pltpu.VMEM((planes + 2 * SHIFT, rows, lanes), jnp.float32),
            ],
        ),
        out_shape=tuple(out_shape),
        compiler_params=pltpu.CompilerParams(vmem_limit_bytes=VMEM),
    )(meta, *operands)


def spread_body(taps_ref, order_ref, kernel_ref, rowsum_ref):
    total = order_ref.shape[1]
    frame = iota((total, total), 0)
    lag = frame - jnp.broadcast_to(order_ref[0:1, :], (total, total))
    value = jnp.zeros((total, total), jnp.float32)
    for tap in range(TAPS):
        value = jnp.where(lag == tap, taps_ref[tap], value)
    small = value.astype(jnp.bfloat16)
    rowsum = jnp.sum(small.astype(jnp.float32), axis=1, keepdims=True) * (1.0 / total)
    rowsum_ref[...] = jnp.broadcast_to(rowsum[:, :, None], (total, SUB, LANES)).reshape(total * SUB, LANES)
    repeat = iota((total, total * SUB), 1) // SUB == iota((total, total * SUB), 0)
    wide = dot(small, repeat.astype(jnp.float32).astype(jnp.bfloat16))
    tall = jnp.broadcast_to(wide[:, None, :], (total, SUB, total * SUB)).reshape(total * SUB, total * SUB)
    same = iota(tall.shape, 0) % SUB == iota(tall.shape, 1) % SUB
    kernel_ref[...] = jnp.where(same, tall, 0.0).astype(jnp.bfloat16)


def spread_kernel(taps, order):
    total = order.shape[1]
    return pl.pallas_call(
        spread_body,
        in_specs=[pl.BlockSpec(memory_space=pltpu.SMEM), pl.BlockSpec(memory_space=pltpu.VMEM)],
        out_shape=(
            jax.ShapeDtypeStruct((total * SUB, total * SUB), jnp.bfloat16),
            jax.ShapeDtypeStruct((total * SUB, LANES), jnp.float32),
        ),
        compiler_params=pltpu.CompilerParams(vmem_limit_bytes=VMEM),
        name="spread_kernel",
    )(taps, order)


def filter_body(group, kernel_ref, rowsum_ref, *refs):
    *got, out_ref = refs
    owners = got[0].shape[0]
    total, _, strip, lanes = out_ref.shape
    frames = group * (total // owners)
    width = frames * SUB
    reach = -(-TAPS // frames)

    for pair in range(strip // (2 * SUB)):
        tiles = []
        for j in range(owners // group):
            halves = []
            for half in range(2):
                low = (2 * pair + half) * SUB
                parts = []
                for ref, count in zip(got, CHUNKS):
                    part = ref[group * j : group * (j + 1), 0:count, 0, low : low + SUB, :]
                    parts.append(part.reshape(group * count * SUB, lanes))
                halves.append(jnp.concatenate(parts, axis=0))
            tiles.append(jnp.concatenate(halves, axis=1))
        mean = sum(jnp.sum(t.astype(jnp.float32).reshape(frames, SUB, 2 * lanes), axis=0) for t in tiles)
        for i in range(len(tiles)):
            lowest = max(0, i - reach)
            rows = slice(i * width, (i + 1) * width)
            value = None
            for j in range(lowest, i + 1):
                part = dot(kernel_ref[rows, j * width : (j + 1) * width], tiles[j])
                value = part if value is None else value + part
            rowsum = rowsum_ref[rows, :].reshape(frames, SUB, lanes)
            value = value.reshape(frames, SUB, 2 * lanes)
            done = [
                value[:, :, h * lanes : (h + 1) * lanes] - rowsum * mean[None, :, h * lanes : (h + 1) * lanes]
                for h in range(2)
            ]
            both = jnp.concatenate(done, axis=1).astype(jnp.bfloat16)
            out_ref[i * frames : (i + 1) * frames, 0, 2 * SUB * pair : 2 * SUB * (pair + 1), :] = both


def filter_frames(kernel, rowsum, got, total, group):
    owners, _, planes, strip, lanes = got[0].shape
    in_specs = [
        pl.BlockSpec(kernel.shape, lambda z: (0, 0)),
        pl.BlockSpec(rowsum.shape, lambda z: (0, 0)),
    ]
    for part in got:
        in_specs.append(pl.BlockSpec((owners, part.shape[1], 1, strip, lanes), lambda z: (0, 0, z, 0, 0)))

    def body(*refs):
        filter_body(group, *refs)

    return pl.pallas_call(
        body,
        grid=(planes,),
        in_specs=in_specs,
        out_specs=pl.BlockSpec((total, 1, strip, lanes), lambda z: (0, z, 0, 0)),
        out_shape=jax.ShapeDtypeStruct((total, planes, strip, lanes), jnp.bfloat16),
        compiler_params=pltpu.CompilerParams(vmem_limit_bytes=VMEM),
        name="filter_frames",
    )(kernel, rowsum, *got)


def local(raw, offsets, taps):
    frame_dev, _, _, _ = raw.shape
    owners = lax.axis_size("frames")
    tiles = lax.axis_size("tiles")
    total = frame_dev * owners
    group = min(owners, 4)

    first_columns, last_columns = pack_edges(raw)
    upward = [(i, i + 1) for i in range(tiles - 1)]
    left = lax.ppermute(last_columns, "tiles", upward)
    right = lax.ppermute(first_columns, "tiles", [(j, i) for i, j in upward])

    tile = lax.axis_index("tiles")
    ends = jnp.stack([tile == 0, tile == tiles - 1]).astype(jnp.int32)
    meta = jnp.concatenate([offsets.reshape(-1), ends])

    order = []
    for block in range(owners // group):
        low = 0
        for count in CHUNKS:
            for owner in range(group * block, group * (block + 1)):
                order += [owner * frame_dev + low + f for f in range(count)]
            low += count
    kernel, rowsum = spread_kernel(taps, jnp.tile(jnp.array(order, jnp.int32)[None], (SUB, 1)))

    got = []
    summed = None
    low = 0
    for count in CHUNKS:
        sent, summed = register(raw, left, right, meta, summed, low, count, owners)
        got.append(lax.all_to_all(sent, "frames", split_axis=0, concat_axis=0, tiled=True))
        low += count
    template = summed_over_frames(summed, owners) * (1.0 / total)
    return filter_frames(kernel, rowsum, got, total, group), template


def summed_over_frames(value, owners):
    planes, rows, lanes = value.shape
    ring = owners // 4
    value = value.reshape(planes, ring, 2, 2, rows // owners, lanes)
    index = lax.axis_index("frames")

    def block(array, axis, at):
        return lax.dynamic_index_in_dim(array, at, axis, keepdims=False)

    core = index % 2
    other = lax.ppermute(block(value, 3, 1 - core), "frames", [(i, i ^ 1) for i in range(owners)])
    value = block(value, 3, core) + other
    pair = index // 2 % 2
    sent = block(value, 2, 1 - pair).astype(jnp.bfloat16)
    other = lax.ppermute(sent, "frames", [(i, i ^ 2) for i in range(owners)])
    value = block(value, 2, pair) + other.astype(jnp.float32)
    place = index // 4
    whole = block(value, 1, place)
    for turn in range(1, ring):
        sent = block(value, 1, (place + turn) % ring).astype(jnp.bfloat16)
        other = lax.ppermute(sent, "frames", [(i, (i + 4 * turn) % owners) for i in range(owners)])
        whole = whole + other.astype(jnp.float32)
    return whole


def solution(mesh):
    placed = (P("frames", None, None, "tiles"), P("frames", None), P())
    return jax.shard_map(
        local,
        mesh=mesh,
        in_specs=placed,
        out_specs=(P(None, None, "frames", "tiles"), P(None, "frames", "tiles")),
        check_vma=False,
    )
```

```python
import jax
import jax.numpy as jnp
from jax import lax
from jax.experimental import pallas as pl
from jax.experimental.pallas import tpu as pltpu
from jax.sharding import PartitionSpec as P


TAPS = 64
SHIFT = 3
RADIUS = 8
HALO = SHIFT + 1
BOX = 2 * RADIUS + 1
LANES = 128
SUB = 8
CHUNKS = (2, 6)
PACK = LANES // (8 * HALO)
VMEM = 56 << 20


def iota(shape, dim):
    return lax.broadcasted_iota(jnp.int32, shape, dim)


def dot(a, b):
    return jnp.dot(a, b, preferred_element_type=jnp.float32)


def pack_body(*refs):
    *raw_refs, first_ref, last_ref, pick = refs
    step = pl.program_id(0)
    planes, _, lanes = raw_refs[0].shape[1:]
    half = lax.rem(step, PACK // len(raw_refs))

    @pl.when(step == 0)
    def _():
        pick[...] = jnp.zeros(pick.shape, pick.dtype)

    low, lane = iota((SUB, LANES), 0), iota((SUB, LANES), 1)
    wide = []
    for f, raw_ref in enumerate(raw_refs):
        for z in range(planes):
            start = ((half * len(raw_refs) + f) * planes + z) * HALO
            head = (low < HALO) & (lane == start + low)
            tail = (low >= SUB - HALO) & (lane == start + low - (SUB - HALO))
            row = (f * planes + z) * lanes
            pick[row : row + SUB, :LANES] = head.astype(jnp.float32).astype(jnp.bfloat16)
            pick[row + lanes - SUB : row + lanes, LANES:] = tail.astype(jnp.float32).astype(jnp.bfloat16)
            wide.append(raw_ref[0, z])
    edges = dot(jnp.concatenate(wide, axis=1), pick[...]).astype(jnp.bfloat16)

    @pl.when(half == 0)
    def _():
        first_ref[0] = edges[:, :LANES]
        last_ref[0] = edges[:, LANES:]

    @pl.when(half != 0)
    def _():
        first_ref[0] += edges[:, :LANES]
        last_ref[0] += edges[:, LANES:]


def pack_edges(raw):
    frames, planes, rows, lanes = raw.shape
    each = 2
    edge = jax.ShapeDtypeStruct((frames // PACK, rows, LANES), jnp.bfloat16)
    spec = pl.BlockSpec((1, rows, LANES), lambda i: (i * each // PACK, 0, 0))
    return pl.pallas_call(
        pack_body,
        grid=(frames // each,),
        in_specs=[
            pl.BlockSpec((1, planes, rows, lanes), lambda i, f=f: (i * each + f, 0, 0, 0)) for f in range(each)
        ],
        out_specs=(spec, spec),
        out_shape=(edge, edge),
        scratch_shapes=[pltpu.VMEM((each * planes * lanes, 2 * LANES), jnp.bfloat16)],
        compiler_params=pltpu.CompilerParams(vmem_limit_bytes=VMEM),
        name="pack_edges",
    )(*[raw] * each)


def high_pass(out_row, in_row, off_y, rows):
    smoothed = 0.0
    for delta, weight in ((-1, 1.0), (1, 1.0), (0, 2.0)):
        reached = out_row + delta
        source = reached - off_y
        inside = (reached >= 0) & (reached < rows) & (source >= 0) & (source < rows)
        gap = jnp.abs(in_row - source)
        term = jnp.where(gap == 0, BOX - 1.0, jnp.where(gap <= RADIUS, -1.0, 0.0))
        term = jnp.where(inside, term, 0.0)
        smoothed = smoothed + weight * term
    return smoothed, term


def high_pass_inside(out_row, in_row, off_y):
    gap = jnp.abs(in_row - out_row + off_y)
    plain = jnp.where(gap == 0, BOX - 1.0, jnp.where(gap <= RADIUS, -1.0, 0.0))
    far = jnp.where(gap <= RADIUS - 1, -4.0, jnp.where(gap == RADIUS, -3.0, jnp.where(gap == RADIUS + 1, -1.0, 0.0)))
    smoothed = jnp.where(gap == 0, 2.0 * BOX - 4.0, jnp.where(gap == 1, BOX - 4.0, far))
    return smoothed, plain


def register_body(first, count, total, meta_ref, raw_ref, left_ref, right_ref, *rest):
    if first > 0:
        sum_in_ref, *rest = rest
    send_ref, sum_out_ref, *rest = rest
    smooth_y, plain_y, split, plain, smooth, summed = rest
    planes, rows, lanes = raw_ref.shape[1:]
    blocks = send_ref.shape[0]
    strip = rows // blocks
    step = pl.program_id(0)

    @pl.when(step == 0)
    def _():
        smooth_y[...] = jnp.zeros(smooth_y.shape, smooth_y.dtype)
        plain_y[...] = jnp.zeros(plain_y.shape, plain_y.dtype)
        smooth[0:HALO] = jnp.zeros((HALO, rows, lanes), jnp.float32)
        smooth[HALO + planes :] = jnp.zeros((HALO, rows, lanes), jnp.float32)
        if first > 0:
            summed[SHIFT : SHIFT + planes] = sum_in_ref[...] * BOX
        else:
            summed[SHIFT : SHIFT + planes] = jnp.zeros((planes, rows, lanes), jnp.float32)

    def frame():
        index = first + step
        off_z, off_y, off_x = meta_ref[3 * index], meta_ref[3 * index + 1], meta_ref[3 * index + 2]
        at_start, at_end = meta_ref[3 * total], meta_ref[3 * total + 1]

        def put(low, tall, lane, pair):
            smoothed, unsmoothed = (value.astype(jnp.bfloat16) for value in pair)
            wide = unsmoothed.shape[1]
            smooth_y[low : low + tall, lane : lane + wide] = smoothed
            smooth_y[low : low + tall, rows + lane : rows + lane + wide] = smoothed
            plain_y[low : low + tall, lane : lane + wide] = unsmoothed

        tall, wide, edge = 64, min(2 * LANES, rows), 16
        for low in range(0, rows, tall):
            lane = min(max((low - RADIUS - HALO) // LANES, 0) * LANES, rows - wide)
            out_row, in_row = iota((tall, wide), 0) + low, iota((tall, wide), 1) + lane
            put(low, tall, lane, high_pass_inside(out_row, in_row, off_y))
        for low, lane in ((0, 0), (rows - edge, rows - wide)):
            out_row, in_row = iota((edge, wide), 0) + low, iota((edge, wide), 1) + lane
            put(low, edge, lane, high_pass(out_row, in_row, off_y, rows))

        slot = lax.rem(index, PACK)
        source = iota((2 * LANES, LANES), 0)
        target = iota((2 * LANES, LANES), 1)
        side, lane = source // LANES, source % LANES - slot * planes * HALO
        plane, column = lane // HALO, lane % HALO
        chosen = (lane >= 0) & (lane < planes * HALO) & (target == plane * 2 * HALO + side * HALO + column)
        pick = chosen.astype(jnp.float32).astype(jnp.bfloat16)
        edges = dot(jnp.concatenate([left_ref[0], right_ref[0]], axis=1), pick).astype(jnp.bfloat16)

        def across(source):
            column = iota(source.shape, 1)
            second = column >= lanes
            column = jnp.where(second, column - lanes, column)
            gap = source - column + off_x
            low = jnp.where(second | ((column == 0) & (at_start > 0)), 0.0, 1.0)
            high = jnp.where(second | ((column == lanes - 1) & (at_end > 0)), 0.0, 1.0)
            middle = jnp.where(second, 1.0, 2.0)
            return jnp.where(gap == 0, middle, jnp.where(gap == -1, low, jnp.where(gap == 1, high, 0.0)))

        inner = across(iota((lanes, 2 * lanes), 0)).astype(jnp.bfloat16)
        outer = iota((2 * HALO, 2 * lanes), 0)
        outer = across(jnp.where(outer < HALO, outer - HALO, outer - HALO + lanes))

        for pair in range(planes // 2):
            for half in range(2):
                z = 2 * pair + half
                pieces = [outer]
                if z > 0:
                    pieces.insert(0, jnp.zeros((2 * HALO * z, 2 * lanes), jnp.float32))
                left_over = LANES - 2 * HALO * (z + 1)
                pieces.append(jnp.zeros((left_over, 2 * lanes), jnp.float32))
                weights = jnp.concatenate([inner, jnp.concatenate(pieces, axis=0).astype(jnp.bfloat16)], axis=0)
                moved = dot(jnp.concatenate([raw_ref[0, z], edges], axis=1), weights)
                big = moved[:, :lanes].astype(jnp.bfloat16)
                columns = slice(half * lanes, (half + 1) * lanes)
                split[:rows, columns] = big
                split[rows:, columns] = (moved[:, :lanes] - big.astype(jnp.float32)).astype(jnp.bfloat16)
                plain[:, columns] = moved[:, lanes:].astype(jnp.bfloat16)
            smoothed = dot(smooth_y[...], split[...])
            shifted = dot(plain_y[...], plain[...])
            for half in range(2):
                z = 2 * pair + half
                columns = slice(half * lanes, (half + 1) * lanes)
                smooth[HALO + z] = smoothed[:, columns]
                summed[SHIFT + z + off_z] += shifted[:, columns]

        def along(block, carry):
            low = pl.multiple_of(block * strip, strip)
            plane = [smooth[HALO + z - off_z, pl.ds(low, strip), :] for z in range(planes)]
            for z in range(planes):
                value = 2.0 * plane[z]
                if z > 0:
                    value = value + plane[z - 1]
                if z + 1 < planes:
                    value = value + plane[z + 1]
                send_ref[block, 0, z] = (value * (1.0 / (BOX * 64))).astype(jnp.bfloat16)
            return carry

        lax.fori_loop(0, blocks, along, 0)

    frame()

    @pl.when(step == count - 1)
    def _():
        sum_out_ref[...] = summed[SHIFT : SHIFT + planes] * (1.0 / BOX)


def register(raw, left, right, meta, summed, first, count, owners):
    frames, planes, rows, lanes = raw.shape

    edge_spec = pl.BlockSpec((1, rows, LANES), lambda f, m: ((first + f) // PACK, 0, 0))
    whole = pl.BlockSpec((planes, rows, lanes), lambda f, m: (0, 0, 0))
    raw_spec = pl.BlockSpec((1, planes, rows, lanes), lambda f, m: (first + f, 0, 0, 0))
    in_specs = [raw_spec, edge_spec, edge_spec]
    operands = [raw, left, right]
    if first > 0:
        in_specs.append(whole)
        operands.append(summed)
    strip = rows // owners
    out_specs = [pl.BlockSpec((owners, 1, planes, strip, lanes), lambda f, m: (0, f, 0, 0, 0))]
    out_shape = [jax.ShapeDtypeStruct((owners, count, planes, strip, lanes), jnp.bfloat16)]
    out_specs.append(whole)
    out_shape.append(jax.ShapeDtypeStruct((planes, rows, lanes), jnp.float32))

    def body(*refs):
        register_body(first, count, frames, *refs)

    return pl.pallas_call(
        body,
        grid_spec=pltpu.PrefetchScalarGridSpec(
            num_scalar_prefetch=1,
            grid=(count,),
            in_specs=in_specs,
            out_specs=tuple(out_specs),
            scratch_shapes=[
                pltpu.VMEM((rows, 2 * rows), jnp.bfloat16),
                pltpu.VMEM((rows, rows), jnp.bfloat16),
                pltpu.VMEM((2 * rows, 2 * lanes), jnp.bfloat16),
                pltpu.VMEM((rows, 2 * lanes), jnp.bfloat16),
                pltpu.VMEM((planes + 2 * HALO, rows, lanes), jnp.float32),
                pltpu.VMEM((planes + 2 * SHIFT, rows, lanes), jnp.float32),
            ],
        ),
        out_shape=tuple(out_shape),
        compiler_params=pltpu.CompilerParams(vmem_limit_bytes=VMEM),
    )(meta, *operands)


def spread_body(taps_ref, order_ref, kernel_ref, rowsum_ref):
    total = order_ref.shape[1]
    frame = iota((total, total), 0)
    lag = frame - jnp.broadcast_to(order_ref[0:1, :], (total, total))
    value = jnp.zeros((total, total), jnp.float32)
    for tap in range(TAPS):
        value = jnp.where(lag == tap, taps_ref[tap], value)
    small = value.astype(jnp.bfloat16)
    rowsum = jnp.sum(small.astype(jnp.float32), axis=1, keepdims=True) * (1.0 / total)
    rowsum_ref[...] = jnp.broadcast_to(rowsum[:, :, None], (total, SUB, LANES)).reshape(total * SUB, LANES)
    repeat = iota((total, total * SUB), 1) // SUB == iota((total, total * SUB), 0)
    wide = dot(small, repeat.astype(jnp.float32).astype(jnp.bfloat16))
    tall = jnp.broadcast_to(wide[:, None, :], (total, SUB, total * SUB)).reshape(total * SUB, total * SUB)
    same = iota(tall.shape, 0) % SUB == iota(tall.shape, 1) % SUB
    kernel_ref[...] = jnp.where(same, tall, 0.0).astype(jnp.bfloat16)


def spread_kernel(taps, order):
    total = order.shape[1]
    return pl.pallas_call(
        spread_body,
        in_specs=[pl.BlockSpec(memory_space=pltpu.SMEM), pl.BlockSpec(memory_space=pltpu.VMEM)],
        out_shape=(
            jax.ShapeDtypeStruct((total * SUB, total * SUB), jnp.bfloat16),
            jax.ShapeDtypeStruct((total * SUB, LANES), jnp.float32),
        ),
        compiler_params=pltpu.CompilerParams(vmem_limit_bytes=VMEM),
        name="spread_kernel",
    )(taps, order)


def filter_body(group, kernel_ref, rowsum_ref, *refs):
    *got, out_ref = refs
    owners = got[0].shape[0]
    total, _, strip, lanes = out_ref.shape
    frames = group * (total // owners)
    width = frames * SUB
    reach = -(-TAPS // frames)

    for pair in range(strip // (2 * SUB)):
        tiles = []
        for j in range(owners // group):
            halves = []
            for half in range(2):
                low = (2 * pair + half) * SUB
                parts = []
                for ref, count in zip(got, CHUNKS):
                    part = ref[group * j : group * (j + 1), 0:count, 0, low : low + SUB, :]
                    parts.append(part.reshape(group * count * SUB, lanes))
                halves.append(jnp.concatenate(parts, axis=0))
            tiles.append(jnp.concatenate(halves, axis=1))
        mean = sum(jnp.sum(t.astype(jnp.float32).reshape(frames, SUB, 2 * lanes), axis=0) for t in tiles)
        for i in range(len(tiles)):
            lowest = max(0, i - reach)
            rows = slice(i * width, (i + 1) * width)
            value = None
            for j in range(lowest, i + 1):
                part = dot(kernel_ref[rows, j * width : (j + 1) * width], tiles[j])
                value = part if value is None else value + part
            rowsum = rowsum_ref[rows, :].reshape(frames, SUB, lanes)
            value = value.reshape(frames, SUB, 2 * lanes)
            done = [
                value[:, :, h * lanes : (h + 1) * lanes] - rowsum * mean[None, :, h * lanes : (h + 1) * lanes]
                for h in range(2)
            ]
            both = jnp.concatenate(done, axis=1).astype(jnp.bfloat16)
            out_ref[i * frames : (i + 1) * frames, 0, 2 * SUB * pair : 2 * SUB * (pair + 1), :] = both


def filter_frames(kernel, rowsum, got, total, group):
    owners, _, planes, strip, lanes = got[0].shape
    in_specs = [
        pl.BlockSpec(kernel.shape, lambda z: (0, 0)),
        pl.BlockSpec(rowsum.shape, lambda z: (0, 0)),
    ]
    for part in got:
        in_specs.append(pl.BlockSpec((owners, part.shape[1], 1, strip, lanes), lambda z: (0, 0, z, 0, 0)))

    def body(*refs):
        filter_body(group, *refs)

    return pl.pallas_call(
        body,
        grid=(planes,),
        in_specs=in_specs,
        out_specs=pl.BlockSpec((total, 1, strip, lanes), lambda z: (0, z, 0, 0)),
        out_shape=jax.ShapeDtypeStruct((total, planes, strip, lanes), jnp.bfloat16),
        compiler_params=pltpu.CompilerParams(vmem_limit_bytes=VMEM),
        name="filter_frames",
    )(kernel, rowsum, *got)


def local(raw, offsets, taps):
    frame_dev, _, _, _ = raw.shape
    owners = lax.axis_size("frames")
    tiles = lax.axis_size("tiles")
    total = frame_dev * owners
    group = min(owners, 4)

    first_columns, last_columns = pack_edges(raw)
    upward = [(i, i + 1) for i in range(tiles - 1)]
    left = lax.ppermute(last_columns, "tiles", upward)
    right = lax.ppermute(first_columns, "tiles", [(j, i) for i, j in upward])

    tile = lax.axis_index("tiles")
    ends = jnp.stack([tile == 0, tile == tiles - 1]).astype(jnp.int32)
    meta = jnp.concatenate([offsets.reshape(-1), ends])

    order = []
    for block in range(owners // group):
        low = 0
        for count in CHUNKS:
            for owner in range(group * block, group * (block + 1)):
                order += [owner * frame_dev + low + f for f in range(count)]
            low += count
    kernel, rowsum = spread_kernel(taps, jnp.tile(jnp.array(order, jnp.int32)[None], (SUB, 1)))

    got = []
    summed = None
    low = 0
    for count in CHUNKS:
        sent, summed = register(raw, left, right, meta, summed, low, count, owners)
        got.append(lax.all_to_all(sent, "frames", split_axis=0, concat_axis=0, tiled=True))
        low += count
    template = summed_over_frames(summed, owners) * (1.0 / total)
    return filter_frames(kernel, rowsum, got, total, group), template


def summed_over_frames(value, owners):
    planes, rows, lanes = value.shape
    chips = owners // 2
    value = value.reshape(planes, chips, 2, rows // owners, lanes)
    index = lax.axis_index("frames")
    chip, core = lax.shift_right_logical(index, 1), lax.bitwise_and(index, 1)

    def block(array, axis, at):
        return lax.dynamic_index_in_dim(array, at, axis, keepdims=False)

    other = lax.ppermute(block(value, 2, 1 - core), "frames", [(i, i ^ 1) for i in range(owners)])
    value = block(value, 2, core) + other
    whole = block(value, 1, chip)
    for turn in range(1, chips):
        to = lax.bitwise_and(chip + turn, chips - 1)
        sent = block(value, 1, to).astype(jnp.bfloat16)
        other = lax.ppermute(sent, "frames", [(i, (i + 2 * turn) % owners) for i in range(owners)])
        whole = whole + other.astype(jnp.float32)
    return whole


def solution(mesh):
    placed = (P("frames", None, None, "tiles"), P("frames", None), P())
    return jax.shard_map(
        local,
        mesh=mesh,
        in_specs=placed,
        out_specs=(P(None, None, "frames", "tiles"), P(None, "frames", "tiles")),
        check_vma=False,
    )
```

```python
import jax
import jax.numpy as jnp
from jax import lax
from jax.experimental import pallas as pl
from jax.experimental.pallas import tpu as pltpu
from jax.sharding import PartitionSpec as P


TAPS = 64
SHIFT = 3
RADIUS = 8
HALO = SHIFT + 1
BOX = 2 * RADIUS + 1
LANES = 128
SUB = 8
CHUNKS = (2, 6)
PACK = LANES // (8 * HALO)
VMEM = 56 << 20


def iota(shape, dim):
    return lax.broadcasted_iota(jnp.int32, shape, dim)


def dot(a, b):
    return jnp.dot(a, b, preferred_element_type=jnp.float32)


def pack_body(*refs):
    *raw_refs, first_ref, last_ref, pick = refs
    step = pl.program_id(0)
    planes, _, lanes = raw_refs[0].shape[1:]
    half = lax.rem(step, PACK // len(raw_refs))

    @pl.when(step == 0)
    def _():
        pick[...] = jnp.zeros(pick.shape, pick.dtype)

    low, lane = iota((SUB, LANES), 0), iota((SUB, LANES), 1)
    wide = []
    for f, raw_ref in enumerate(raw_refs):
        for z in range(planes):
            start = ((half * len(raw_refs) + f) * planes + z) * HALO
            head = (low < HALO) & (lane == start + low)
            tail = (low >= SUB - HALO) & (lane == start + low - (SUB - HALO))
            row = (f * planes + z) * lanes
            pick[row : row + SUB, :LANES] = head.astype(jnp.float32).astype(jnp.bfloat16)
            pick[row + lanes - SUB : row + lanes, LANES:] = tail.astype(jnp.float32).astype(jnp.bfloat16)
            wide.append(raw_ref[0, z])
    edges = dot(jnp.concatenate(wide, axis=1), pick[...]).astype(jnp.bfloat16)

    @pl.when(half == 0)
    def _():
        first_ref[0] = edges[:, :LANES]
        last_ref[0] = edges[:, LANES:]

    @pl.when(half != 0)
    def _():
        first_ref[0] += edges[:, :LANES]
        last_ref[0] += edges[:, LANES:]


def pack_edges(raw):
    frames, planes, rows, lanes = raw.shape
    each = 2
    edge = jax.ShapeDtypeStruct((frames // PACK, rows, LANES), jnp.bfloat16)
    spec = pl.BlockSpec((1, rows, LANES), lambda i: (i * each // PACK, 0, 0))
    return pl.pallas_call(
        pack_body,
        grid=(frames // each,),
        in_specs=[
            pl.BlockSpec((1, planes, rows, lanes), lambda i, f=f: (i * each + f, 0, 0, 0)) for f in range(each)
        ],
        out_specs=(spec, spec),
        out_shape=(edge, edge),
        scratch_shapes=[pltpu.VMEM((each * planes * lanes, 2 * LANES), jnp.bfloat16)],
        compiler_params=pltpu.CompilerParams(vmem_limit_bytes=VMEM),
        name="pack_edges",
    )(*[raw] * each)


def high_pass(out_row, in_row, off_y, rows):
    smoothed = 0.0
    for delta, weight in ((-1, 1.0), (1, 1.0), (0, 2.0)):
        reached = out_row + delta
        source = reached - off_y
        inside = (reached >= 0) & (reached < rows) & (source >= 0) & (source < rows)
        gap = jnp.abs(in_row - source)
        term = jnp.where(gap == 0, BOX - 1.0, jnp.where(gap <= RADIUS, -1.0, 0.0))
        term = jnp.where(inside, term, 0.0)
        smoothed = smoothed + weight * term
    return smoothed, term


def high_pass_inside(out_row, in_row, off_y):
    gap = jnp.abs(in_row - out_row + off_y)
    plain = jnp.where(gap == 0, BOX - 1.0, jnp.where(gap <= RADIUS, -1.0, 0.0))
    far = jnp.where(gap <= RADIUS - 1, -4.0, jnp.where(gap == RADIUS, -3.0, jnp.where(gap == RADIUS + 1, -1.0, 0.0)))
    smoothed = jnp.where(gap == 0, 2.0 * BOX - 4.0, jnp.where(gap == 1, BOX - 4.0, far))
    return smoothed, plain


def fill_rows(off_y, rows, put):
    tall, wide, edge = 64, min(2 * LANES, rows), 16
    for low in range(0, rows, tall):
        lane = min(max((low - RADIUS - HALO) // LANES, 0) * LANES, rows - wide)
        out_row, in_row = iota((tall, wide), 0) + low, iota((tall, wide), 1) + lane
        put(low, lane, *high_pass_inside(out_row, in_row, off_y))
    for low, lane in ((0, 0), (rows - edge, rows - wide)):
        out_row, in_row = iota((edge, wide), 0) + low, iota((edge, wide), 1) + lane
        put(low, lane, *high_pass(out_row, in_row, off_y, rows))


def edge_columns(left, right, slot, planes):
    source = iota((2 * LANES, LANES), 0)
    target = iota((2 * LANES, LANES), 1)
    side, lane = source // LANES, source % LANES - slot * planes * HALO
    plane, column = lane // HALO, lane % HALO
    chosen = (lane >= 0) & (lane < planes * HALO) & (target == plane * 2 * HALO + side * HALO + column)
    pick = chosen.astype(jnp.float32).astype(jnp.bfloat16)
    return dot(jnp.concatenate([left, right], axis=1), pick).astype(jnp.bfloat16)


def column_weights(planes, lanes, off_x, weigh):
    def across(source):
        column = iota(source.shape, 1)
        return weigh(source - column + off_x, column)

    inner = across(iota((lanes, lanes), 0)).astype(jnp.bfloat16)
    outer = iota((2 * HALO, lanes), 0)
    outer = across(jnp.where(outer < HALO, outer - HALO, outer - HALO + lanes))
    weights = []
    for z in range(planes):
        pieces = [outer]
        if z > 0:
            pieces.insert(0, jnp.zeros((2 * HALO * z, lanes), jnp.float32))
        pieces.append(jnp.zeros((LANES - 2 * HALO * (z + 1), lanes), jnp.float32))
        weights.append(jnp.concatenate([inner, jnp.concatenate(pieces, axis=0).astype(jnp.bfloat16)], axis=0))
    return weights


def register_body(first, total, meta_ref, raw_ref, left_ref, right_ref, send_ref, smooth_y, split, smooth):
    planes, rows, lanes = raw_ref.shape[1:]
    blocks = send_ref.shape[0]
    strip = rows // blocks
    step = pl.program_id(0)

    @pl.when(step == 0)
    def _():
        smooth_y[...] = jnp.zeros(smooth_y.shape, smooth_y.dtype)
        smooth[0:HALO] = jnp.zeros((HALO, rows, lanes), jnp.float32)
        smooth[HALO + planes :] = jnp.zeros((HALO, rows, lanes), jnp.float32)

    index = first + step
    off_z, off_y, off_x = meta_ref[3 * index], meta_ref[3 * index + 1], meta_ref[3 * index + 2]
    at_start, at_end = meta_ref[3 * total], meta_ref[3 * total + 1]

    def put(low, lane, smoothed, unsmoothed):
        smoothed = smoothed.astype(jnp.bfloat16)
        tall, wide = smoothed.shape
        smooth_y[low : low + tall, lane : lane + wide] = smoothed
        smooth_y[low : low + tall, rows + lane : rows + lane + wide] = smoothed

    fill_rows(off_y, rows, put)
    edges = edge_columns(left_ref[0], right_ref[0], lax.rem(index, PACK), planes)

    def weigh(gap, column):
        low = jnp.where((column == 0) & (at_start > 0), 0.0, 1.0)
        high = jnp.where((column == lanes - 1) & (at_end > 0), 0.0, 1.0)
        return jnp.where(gap == 0, 2.0, jnp.where(gap == -1, low, jnp.where(gap == 1, high, 0.0)))

    weights = column_weights(planes, lanes, off_x, weigh)
    for pair in range(planes // 2):
        for half in range(2):
            z = 2 * pair + half
            moved = dot(jnp.concatenate([raw_ref[0, z], edges], axis=1), weights[z])
            big = moved.astype(jnp.bfloat16)
            columns = slice(half * lanes, (half + 1) * lanes)
            split[:rows, columns] = big
            split[rows:, columns] = (moved - big.astype(jnp.float32)).astype(jnp.bfloat16)
        smoothed = dot(smooth_y[...], split[...])
        for half in range(2):
            smooth[HALO + 2 * pair + half] = smoothed[:, half * lanes : (half + 1) * lanes]

    def along(block, carry):
        low = pl.multiple_of(block * strip, strip)
        plane = [smooth[HALO + z - off_z, pl.ds(low, strip), :] for z in range(planes)]
        for z in range(planes):
            value = 2.0 * plane[z]
            if z > 0:
                value = value + plane[z - 1]
            if z + 1 < planes:
                value = value + plane[z + 1]
            send_ref[block, 0, z] = (value * (1.0 / (BOX * 64))).astype(jnp.bfloat16)
        return carry

    lax.fori_loop(0, blocks, along, 0)


def register(raw, left, right, meta, first, count, owners):
    frames, planes, rows, lanes = raw.shape
    strip = rows // owners
    edge_spec = pl.BlockSpec((1, rows, LANES), lambda f, m: ((first + f) // PACK, 0, 0))

    def body(*refs):
        register_body(first, frames, *refs)

    return pl.pallas_call(
        body,
        grid_spec=pltpu.PrefetchScalarGridSpec(
            num_scalar_prefetch=1,
            grid=(count,),
            in_specs=[
                pl.BlockSpec((1, planes, rows, lanes), lambda f, m: (first + f, 0, 0, 0)),
                edge_spec,
                edge_spec,
            ],
            out_specs=pl.BlockSpec((owners, 1, planes, strip, lanes), lambda f, m: (0, f, 0, 0, 0)),
            scratch_shapes=[
                pltpu.VMEM((rows, 2 * rows), jnp.bfloat16),
                pltpu.VMEM((2 * rows, 2 * lanes), jnp.bfloat16),
                pltpu.VMEM((planes + 2 * HALO, rows, lanes), jnp.float32),
            ],
        ),
        out_shape=jax.ShapeDtypeStruct((owners, count, planes, strip, lanes), jnp.bfloat16),
        compiler_params=pltpu.CompilerParams(vmem_limit_bytes=VMEM),
    )(meta, raw, left, right)


def frame_sum_body(meta_ref, raw_ref, left_ref, right_ref, out_ref, plain_y, plain, summed):
    planes, rows, lanes = raw_ref.shape[1:]
    index = pl.program_id(0)

    @pl.when(index == 0)
    def _():
        plain_y[...] = jnp.zeros(plain_y.shape, plain_y.dtype)
        summed[...] = jnp.zeros(summed.shape, summed.dtype)

    off_z, off_y, off_x = meta_ref[3 * index], meta_ref[3 * index + 1], meta_ref[3 * index + 2]

    def put(low, lane, smoothed, unsmoothed):
        tall, wide = unsmoothed.shape
        plain_y[low : low + tall, lane : lane + wide] = unsmoothed.astype(jnp.bfloat16)

    fill_rows(off_y, rows, put)
    edges = edge_columns(left_ref[0], right_ref[0], lax.rem(index, PACK), planes)
    weights = column_weights(planes, lanes, off_x, lambda gap, column: jnp.where(gap == 0, 1.0, 0.0))
    for pair in range(planes // 2):
        for half in range(2):
            z = 2 * pair + half
            moved = dot(jnp.concatenate([raw_ref[0, z], edges], axis=1), weights[z])
            plain[:, half * lanes : (half + 1) * lanes] = moved.astype(jnp.bfloat16)
        shifted = dot(plain_y[...], plain[...])
        for half in range(2):
            summed[SHIFT + 2 * pair + half + off_z] += shifted[:, half * lanes : (half + 1) * lanes]

    @pl.when(index == pl.num_programs(0) - 1)
    def _():
        out_ref[...] = summed[SHIFT : SHIFT + planes] * (1.0 / BOX)


def frame_sum(raw, left, right, meta):
    frames, planes, rows, lanes = raw.shape
    edge_spec = pl.BlockSpec((1, rows, LANES), lambda f, m: (f // PACK, 0, 0))
    return pl.pallas_call(
        frame_sum_body,
        grid_spec=pltpu.PrefetchScalarGridSpec(
            num_scalar_prefetch=1,
            grid=(frames,),
            in_specs=[pl.BlockSpec((1, planes, rows, lanes), lambda f, m: (f, 0, 0, 0)), edge_spec, edge_spec],
            out_specs=pl.BlockSpec((planes, rows, lanes), lambda f, m: (0, 0, 0)),
            scratch_shapes=[
                pltpu.VMEM((rows, rows), jnp.bfloat16),
                pltpu.VMEM((rows, 2 * lanes), jnp.bfloat16),
                pltpu.VMEM((planes + 2 * SHIFT, rows, lanes), jnp.float32),
            ],
        ),
        out_shape=jax.ShapeDtypeStruct((planes, rows, lanes), jnp.float32),
        compiler_params=pltpu.CompilerParams(vmem_limit_bytes=VMEM),
        name="frame_sum",
    )(meta, raw, left, right)


def spread_body(taps_ref, order_ref, kernel_ref, rowsum_ref):
    total = order_ref.shape[1]
    frame = iota((total, total), 0)
    lag = frame - jnp.broadcast_to(order_ref[0:1, :], (total, total))
    value = jnp.zeros((total, total), jnp.float32)
    for tap in range(TAPS):
        value = jnp.where(lag == tap, taps_ref[tap], value)
    small = value.astype(jnp.bfloat16)
    rowsum = jnp.sum(small.astype(jnp.float32), axis=1, keepdims=True) * (1.0 / total)
    rowsum_ref[...] = jnp.broadcast_to(rowsum[:, :, None], (total, SUB, LANES)).reshape(total * SUB, LANES)
    repeat = iota((total, total * SUB), 1) // SUB == iota((total, total * SUB), 0)
    wide = dot(small, repeat.astype(jnp.float32).astype(jnp.bfloat16))
    tall = jnp.broadcast_to(wide[:, None, :], (total, SUB, total * SUB)).reshape(total * SUB, total * SUB)
    same = iota(tall.shape, 0) % SUB == iota(tall.shape, 1) % SUB
    kernel_ref[...] = jnp.where(same, tall, 0.0).astype(jnp.bfloat16)


def spread_kernel(taps, order):
    total = order.shape[1]
    return pl.pallas_call(
        spread_body,
        in_specs=[pl.BlockSpec(memory_space=pltpu.SMEM), pl.BlockSpec(memory_space=pltpu.VMEM)],
        out_shape=(
            jax.ShapeDtypeStruct((total * SUB, total * SUB), jnp.bfloat16),
            jax.ShapeDtypeStruct((total * SUB, LANES), jnp.float32),
        ),
        compiler_params=pltpu.CompilerParams(vmem_limit_bytes=VMEM),
        name="spread_kernel",
    )(taps, order)


def filter_body(group, kernel_ref, rowsum_ref, *refs):
    *got, out_ref = refs
    owners = got[0].shape[0]
    total, _, strip, lanes = out_ref.shape
    frames = group * (total // owners)
    width = frames * SUB
    reach = -(-TAPS // frames)

    for pair in range(strip // (2 * SUB)):
        tiles = []
        for j in range(owners // group):
            halves = []
            for half in range(2):
                low = (2 * pair + half) * SUB
                parts = []
                for ref, count in zip(got, CHUNKS):
                    part = ref[group * j : group * (j + 1), 0:count, 0, low : low + SUB, :]
                    parts.append(part.reshape(group * count * SUB, lanes))
                halves.append(jnp.concatenate(parts, axis=0))
            tiles.append(jnp.concatenate(halves, axis=1))
        mean = sum(jnp.sum(t.astype(jnp.float32).reshape(frames, SUB, 2 * lanes), axis=0) for t in tiles)
        for i in range(len(tiles)):
            lowest = max(0, i - reach)
            rows = slice(i * width, (i + 1) * width)
            value = None
            for j in range(lowest, i + 1):
                part = dot(kernel_ref[rows, j * width : (j + 1) * width], tiles[j])
                value = part if value is None else value + part
            rowsum = rowsum_ref[rows, :].reshape(frames, SUB, lanes)
            value = value.reshape(frames, SUB, 2 * lanes)
            done = [
                value[:, :, h * lanes : (h + 1) * lanes] - rowsum * mean[None, :, h * lanes : (h + 1) * lanes]
                for h in range(2)
            ]
            both = jnp.concatenate(done, axis=1).astype(jnp.bfloat16)
            out_ref[i * frames : (i + 1) * frames, 0, 2 * SUB * pair : 2 * SUB * (pair + 1), :] = both


def filter_frames(kernel, rowsum, got, total, group):
    owners, _, planes, strip, lanes = got[0].shape
    in_specs = [
        pl.BlockSpec(kernel.shape, lambda z: (0, 0)),
        pl.BlockSpec(rowsum.shape, lambda z: (0, 0)),
    ]
    for part in got:
        in_specs.append(pl.BlockSpec((owners, part.shape[1], 1, strip, lanes), lambda z: (0, 0, z, 0, 0)))

    def body(*refs):
        filter_body(group, *refs)

    return pl.pallas_call(
        body,
        grid=(planes,),
        in_specs=in_specs,
        out_specs=pl.BlockSpec((total, 1, strip, lanes), lambda z: (0, z, 0, 0)),
        out_shape=jax.ShapeDtypeStruct((total, planes, strip, lanes), jnp.bfloat16),
        compiler_params=pltpu.CompilerParams(vmem_limit_bytes=VMEM),
        name="filter_frames",
    )(kernel, rowsum, *got)


def local(raw, offsets, taps):
    frame_dev, _, _, _ = raw.shape
    owners = lax.axis_size("frames")
    tiles = lax.axis_size("tiles")
    total = frame_dev * owners
    group = min(owners, 4)

    first_columns, last_columns = pack_edges(raw)
    upward = [(i, i + 1) for i in range(tiles - 1)]
    left = lax.ppermute(last_columns, "tiles", upward)
    right = lax.ppermute(first_columns, "tiles", [(j, i) for i, j in upward])

    tile = lax.axis_index("tiles")
    ends = jnp.stack([tile == 0, tile == tiles - 1]).astype(jnp.int32)
    meta = jnp.concatenate([offsets.reshape(-1), ends])

    order = []
    for block in range(owners // group):
        low = 0
        for count in CHUNKS:
            for owner in range(group * block, group * (block + 1)):
                order += [owner * frame_dev + low + f for f in range(count)]
            low += count
    kernel, rowsum = spread_kernel(taps, jnp.tile(jnp.array(order, jnp.int32)[None], (SUB, 1)))

    got = []
    low = 0
    for count in CHUNKS:
        sent = register(raw, left, right, meta, low, count, owners)
        got.append(lax.all_to_all(sent, "frames", split_axis=0, concat_axis=0, tiled=True))
        low += count
    template = summed_over_frames(frame_sum(raw, left, right, meta), owners) * (1.0 / total)
    return filter_frames(kernel, rowsum, got, total, group), template


def summed_over_frames(value, owners):
    planes, rows, lanes = value.shape
    chips = owners // 2
    value = value.reshape(planes, chips, 2, rows // owners, lanes)
    index = lax.axis_index("frames")
    chip, core = lax.shift_right_logical(index, 1), lax.bitwise_and(index, 1)

    def block(array, axis, at):
        return lax.dynamic_index_in_dim(array, at, axis, keepdims=False)

    other = lax.ppermute(block(value, 2, 1 - core), "frames", [(i, i ^ 1) for i in range(owners)])
    value = block(value, 2, core) + other
    whole = block(value, 1, chip)
    for turn in range(1, chips):
        to = lax.bitwise_and(chip + turn, chips - 1)
        sent = block(value, 1, to).astype(jnp.bfloat16)
        other = lax.ppermute(sent, "frames", [(i, (i + 2 * turn) % owners) for i in range(owners)])
        whole = whole + other.astype(jnp.float32)
    return whole


def solution(mesh):
    placed = (P("frames", None, None, "tiles"), P("frames", None), P())
    return jax.shard_map(
        local,
        mesh=mesh,
        in_specs=placed,
        out_specs=(P(None, None, "frames", "tiles"), P(None, "frames", "tiles")),
        check_vma=False,
    )
```

```python
import jax
import jax.numpy as jnp
from jax import lax
from jax.experimental import pallas as pl
from jax.experimental.pallas import tpu as pltpu
from jax.sharding import PartitionSpec as P


TAPS = 64
SHIFT = 3
RADIUS = 8
HALO = SHIFT + 1
BOX = 2 * RADIUS + 1
LANES = 128
SUB = 8
CHUNKS = (2, 6)
PACK = LANES // (8 * HALO)
VMEM = 56 << 20


def iota(shape, dim):
    return lax.broadcasted_iota(jnp.int32, shape, dim)


def dot(a, b):
    return jnp.dot(a, b, preferred_element_type=jnp.float32)


def pack_body(*refs):
    *raw_refs, first_ref, last_ref, pick = refs
    step = pl.program_id(0)
    planes, _, lanes = raw_refs[0].shape[1:]
    half = lax.rem(step, PACK // len(raw_refs))

    @pl.when(step == 0)
    def _():
        pick[...] = jnp.zeros(pick.shape, pick.dtype)

    low, lane = iota((SUB, LANES), 0), iota((SUB, LANES), 1)
    wide = []
    for f, raw_ref in enumerate(raw_refs):
        for z in range(planes):
            start = ((half * len(raw_refs) + f) * planes + z) * HALO
            head = (low < HALO) & (lane == start + low)
            tail = (low >= SUB - HALO) & (lane == start + low - (SUB - HALO))
            row = (f * planes + z) * lanes
            pick[row : row + SUB, :LANES] = head.astype(jnp.float32).astype(jnp.bfloat16)
            pick[row + lanes - SUB : row + lanes, LANES:] = tail.astype(jnp.float32).astype(jnp.bfloat16)
            wide.append(raw_ref[0, z])
    edges = dot(jnp.concatenate(wide, axis=1), pick[...]).astype(jnp.bfloat16)

    @pl.when(half == 0)
    def _():
        first_ref[0] = edges[:, :LANES]
        last_ref[0] = edges[:, LANES:]

    @pl.when(half != 0)
    def _():
        first_ref[0] += edges[:, :LANES]
        last_ref[0] += edges[:, LANES:]


def pack_edges(raw):
    frames, planes, rows, lanes = raw.shape
    each = 2
    edge = jax.ShapeDtypeStruct((frames // PACK, rows, LANES), jnp.bfloat16)
    spec = pl.BlockSpec((1, rows, LANES), lambda i: (i * each // PACK, 0, 0))
    return pl.pallas_call(
        pack_body,
        grid=(frames // each,),
        in_specs=[
            pl.BlockSpec((1, planes, rows, lanes), lambda i, f=f: (i * each + f, 0, 0, 0)) for f in range(each)
        ],
        out_specs=(spec, spec),
        out_shape=(edge, edge),
        scratch_shapes=[pltpu.VMEM((each * planes * lanes, 2 * LANES), jnp.bfloat16)],
        compiler_params=pltpu.CompilerParams(vmem_limit_bytes=VMEM),
        name="pack_edges",
    )(*[raw] * each)


def high_pass(out_row, in_row, off_y, rows):
    smoothed = 0.0
    for delta, weight in ((-1, 1.0), (1, 1.0), (0, 2.0)):
        reached = out_row + delta
        source = reached - off_y
        inside = (reached >= 0) & (reached < rows) & (source >= 0) & (source < rows)
        gap = jnp.abs(in_row - source)
        term = jnp.where(gap == 0, BOX - 1.0, jnp.where(gap <= RADIUS, -1.0, 0.0))
        term = jnp.where(inside, term, 0.0)
        smoothed = smoothed + weight * term
    return smoothed, term


def high_pass_inside(out_row, in_row, off_y):
    gap = jnp.abs(in_row - out_row + off_y)
    plain = jnp.where(gap == 0, BOX - 1.0, jnp.where(gap <= RADIUS, -1.0, 0.0))
    far = jnp.where(gap <= RADIUS - 1, -4.0, jnp.where(gap == RADIUS, -3.0, jnp.where(gap == RADIUS + 1, -1.0, 0.0)))
    smoothed = jnp.where(gap == 0, 2.0 * BOX - 4.0, jnp.where(gap == 1, BOX - 4.0, far))
    return smoothed, plain


def fill_rows(off_y, rows, put):
    tall, wide, edge = 64, min(2 * LANES, rows), 16
    for low in range(0, rows, tall):
        lane = min(max((low - RADIUS - HALO) // LANES, 0) * LANES, rows - wide)
        out_row, in_row = iota((tall, wide), 0) + low, iota((tall, wide), 1) + lane
        put(low, lane, *high_pass_inside(out_row, in_row, off_y))
    for low, lane in ((0, 0), (rows - edge, rows - wide)):
        out_row, in_row = iota((edge, wide), 0) + low, iota((edge, wide), 1) + lane
        put(low, lane, *high_pass(out_row, in_row, off_y, rows))


def edge_columns(left, right, slot, planes):
    source = iota((2 * LANES, LANES), 0)
    target = iota((2 * LANES, LANES), 1)
    side, lane = source // LANES, source % LANES - slot * planes * HALO
    plane, column = lane // HALO, lane % HALO
    chosen = (lane >= 0) & (lane < planes * HALO) & (target == plane * 2 * HALO + side * HALO + column)
    pick = chosen.astype(jnp.float32).astype(jnp.bfloat16)
    return dot(jnp.concatenate([left, right], axis=1), pick).astype(jnp.bfloat16)


def column_weights(planes, lanes, off_x, weigh):
    def across(source):
        column = iota(source.shape, 1)
        return weigh(source - column + off_x, column)

    inner = across(iota((lanes, lanes), 0)).astype(jnp.bfloat16)
    outer = iota((2 * HALO, lanes), 0)
    outer = across(jnp.where(outer < HALO, outer - HALO, outer - HALO + lanes))
    weights = []
    for z in range(planes):
        pieces = [outer]
        if z > 0:
            pieces.insert(0, jnp.zeros((2 * HALO * z, lanes), jnp.float32))
        pieces.append(jnp.zeros((LANES - 2 * HALO * (z + 1), lanes), jnp.float32))
        weights.append(jnp.concatenate([inner, jnp.concatenate(pieces, axis=0).astype(jnp.bfloat16)], axis=0))
    return weights


def register_body(first, total, meta_ref, raw_ref, left_ref, right_ref, send_ref, smooth_y, split, smooth):
    planes, rows, lanes = raw_ref.shape[1:]
    blocks = send_ref.shape[0]
    strip = rows // blocks
    step = pl.program_id(0)

    @pl.when(step == 0)
    def _():
        smooth_y[...] = jnp.zeros(smooth_y.shape, smooth_y.dtype)
        smooth[0:HALO] = jnp.zeros((HALO, rows, lanes), jnp.float32)
        smooth[HALO + planes :] = jnp.zeros((HALO, rows, lanes), jnp.float32)

    index = first + step
    off_z, off_y, off_x = meta_ref[3 * index], meta_ref[3 * index + 1], meta_ref[3 * index + 2]
    at_start, at_end = meta_ref[3 * total], meta_ref[3 * total + 1]

    def put(low, lane, smoothed, unsmoothed):
        smoothed = smoothed.astype(jnp.bfloat16)
        tall, wide = smoothed.shape
        smooth_y[low : low + tall, lane : lane + wide] = smoothed
        smooth_y[low : low + tall, rows + lane : rows + lane + wide] = smoothed

    fill_rows(off_y, rows, put)
    edges = edge_columns(left_ref[0], right_ref[0], lax.rem(index, PACK), planes)

    def weigh(gap, column):
        low = jnp.where((column == 0) & (at_start > 0), 0.0, 1.0)
        high = jnp.where((column == lanes - 1) & (at_end > 0), 0.0, 1.0)
        return jnp.where(gap == 0, 2.0, jnp.where(gap == -1, low, jnp.where(gap == 1, high, 0.0)))

    weights = column_weights(planes, lanes, off_x, weigh)
    for pair in range(planes // 2):
        for half in range(2):
            z = 2 * pair + half
            moved = dot(jnp.concatenate([raw_ref[0, z], edges], axis=1), weights[z])
            big = moved.astype(jnp.bfloat16)
            columns = slice(half * lanes, (half + 1) * lanes)
            split[:rows, columns] = big
            split[rows:, columns] = (moved - big.astype(jnp.float32)).astype(jnp.bfloat16)
        smoothed = dot(smooth_y[...], split[...])
        for half in range(2):
            smooth[HALO + 2 * pair + half] = smoothed[:, half * lanes : (half + 1) * lanes]

    def along(block, carry):
        low = pl.multiple_of(block * strip, strip)
        plane = [smooth[HALO + z - off_z, pl.ds(low, strip), :] for z in range(planes)]
        for z in range(planes):
            value = 2.0 * plane[z]
            if z > 0:
                value = value + plane[z - 1]
            if z + 1 < planes:
                value = value + plane[z + 1]
            send_ref[block, 0, z] = (value * (1.0 / (BOX * 64))).astype(jnp.bfloat16)
        return carry

    lax.fori_loop(0, blocks, along, 0)


def register(raw, left, right, meta, first, count, owners):
    frames, planes, rows, lanes = raw.shape
    strip = rows // owners
    edge_spec = pl.BlockSpec((1, rows, LANES), lambda f, m: ((first + f) // PACK, 0, 0))

    def body(*refs):
        register_body(first, frames, *refs)

    return pl.pallas_call(
        body,
        grid_spec=pltpu.PrefetchScalarGridSpec(
            num_scalar_prefetch=1,
            grid=(count,),
            in_specs=[
                pl.BlockSpec((1, planes, rows, lanes), lambda f, m: (first + f, 0, 0, 0)),
                edge_spec,
                edge_spec,
            ],
            out_specs=pl.BlockSpec((owners, 1, planes, strip, lanes), lambda f, m: (0, f, 0, 0, 0)),
            scratch_shapes=[
                pltpu.VMEM((rows, 2 * rows), jnp.bfloat16),
                pltpu.VMEM((2 * rows, 2 * lanes), jnp.bfloat16),
                pltpu.VMEM((planes + 2 * HALO, rows, lanes), jnp.float32),
            ],
        ),
        out_shape=jax.ShapeDtypeStruct((owners, count, planes, strip, lanes), jnp.bfloat16),
        compiler_params=pltpu.CompilerParams(vmem_limit_bytes=62 << 20),
    )(meta, raw, left, right)


def frame_sum_body(meta_ref, raw_ref, left_ref, right_ref, out_ref, plain_y, plain, summed):
    planes, rows, lanes = raw_ref.shape[1:]
    index = pl.program_id(0)

    @pl.when(index == 0)
    def _():
        plain_y[...] = jnp.zeros(plain_y.shape, plain_y.dtype)
        summed[...] = jnp.zeros(summed.shape, summed.dtype)

    off_z, off_y, off_x = meta_ref[3 * index], meta_ref[3 * index + 1], meta_ref[3 * index + 2]

    def put(low, lane, smoothed, unsmoothed):
        tall, wide = unsmoothed.shape
        plain_y[low : low + tall, lane : lane + wide] = unsmoothed.astype(jnp.bfloat16)

    fill_rows(off_y, rows, put)
    edges = edge_columns(left_ref[0], right_ref[0], lax.rem(index, PACK), planes)
    weights = column_weights(planes, lanes, off_x, lambda gap, column: jnp.where(gap == 0, 1.0, 0.0))
    for pair in range(planes // 2):
        for half in range(2):
            z = 2 * pair + half
            moved = dot(jnp.concatenate([raw_ref[0, z], edges], axis=1), weights[z])
            plain[:, half * lanes : (half + 1) * lanes] = moved.astype(jnp.bfloat16)
        shifted = dot(plain_y[...], plain[...])
        for half in range(2):
            summed[SHIFT + 2 * pair + half + off_z] += shifted[:, half * lanes : (half + 1) * lanes]

    @pl.when(index == pl.num_programs(0) - 1)
    def _():
        out_ref[...] = summed[SHIFT : SHIFT + planes] * (1.0 / BOX)


def frame_sum(raw, left, right, meta):
    frames, planes, rows, lanes = raw.shape
    edge_spec = pl.BlockSpec((1, rows, LANES), lambda f, m: (f // PACK, 0, 0))
    return pl.pallas_call(
        frame_sum_body,
        grid_spec=pltpu.PrefetchScalarGridSpec(
            num_scalar_prefetch=1,
            grid=(frames,),
            in_specs=[pl.BlockSpec((1, planes, rows, lanes), lambda f, m: (f, 0, 0, 0)), edge_spec, edge_spec],
            out_specs=pl.BlockSpec((planes, rows, lanes), lambda f, m: (0, 0, 0)),
            scratch_shapes=[
                pltpu.VMEM((rows, rows), jnp.bfloat16),
                pltpu.VMEM((rows, 2 * lanes), jnp.bfloat16),
                pltpu.VMEM((planes + 2 * SHIFT, rows, lanes), jnp.float32),
            ],
        ),
        out_shape=jax.ShapeDtypeStruct((planes, rows, lanes), jnp.float32),
        compiler_params=pltpu.CompilerParams(vmem_limit_bytes=VMEM),
        name="frame_sum",
    )(meta, raw, left, right)


def spread_body(taps_ref, order_ref, kernel_ref, rowsum_ref):
    total = rowsum_ref.shape[0] // SUB
    frames = order_ref.shape[1] // 2
    reach = kernel_ref.shape[1] // (frames * SUB) - 1
    for back in range(reach + 1):
        lag = iota((frames, 2 * frames), 0) + (back * frames - order_ref[0:1, :])
        value = jnp.zeros(lag.shape, jnp.float32)
        for tap in range(TAPS):
            value = jnp.where(lag == tap, taps_ref[tap], value)
        small = value.astype(jnp.bfloat16)
        shape = (2 * frames, frames * SUB)
        repeat = iota(shape, 1) // SUB == iota(shape, 0)
        wide = dot(small, repeat.astype(jnp.float32).astype(jnp.bfloat16))
        width = frames * SUB
        tall = jnp.broadcast_to(wide[:, None, :], (frames, SUB, width)).reshape(width, width)
        same = iota(tall.shape, 0) % SUB == iota(tall.shape, 1) % SUB
        low = (reach - back) * width
        kernel_ref[:, low : low + width] = jnp.where(same, tall, 0.0).astype(jnp.bfloat16)

    lag = iota((total, LANES), 0) - iota((total, LANES), 1)
    value = jnp.zeros(lag.shape, jnp.float32)
    for tap in range(TAPS):
        value = jnp.where((lag >= 0) & (iota(lag.shape, 1) == tap), taps_ref[tap], value)
    rowsum = dot(value.astype(jnp.bfloat16), jnp.ones((LANES, LANES), jnp.bfloat16)) * (1.0 / total)
    rowsum_ref[...] = jnp.broadcast_to(rowsum[:, None, :], (total, SUB, LANES)).reshape(total * SUB, LANES)


def spread_kernel(taps, order, total, frames, reach):
    def body(*refs):
        spread_body(*refs)

    return pl.pallas_call(
        body,
        in_specs=[pl.BlockSpec(memory_space=pltpu.SMEM), pl.BlockSpec(memory_space=pltpu.VMEM)],
        out_shape=(
            jax.ShapeDtypeStruct((frames * SUB, (reach + 1) * frames * SUB), jnp.bfloat16),
            jax.ShapeDtypeStruct((total * SUB, LANES), jnp.float32),
        ),
        compiler_params=pltpu.CompilerParams(vmem_limit_bytes=VMEM),
        name="spread_kernel",
    )(taps, order)


def filter_body(group, kernel_ref, rowsum_ref, *refs):
    *got, out_ref = refs
    owners = got[0].shape[0]
    total, _, strip, lanes = out_ref.shape
    frames = group * (total // owners)
    width = frames * SUB
    reach = kernel_ref.shape[1] // width - 1

    for z, pair in [(z, pair) for z in range(out_ref.shape[1]) for pair in range(strip // (2 * SUB))]:
        tiles = []
        for j in range(owners // group):
            halves = []
            for half in range(2):
                low = (2 * pair + half) * SUB
                parts = []
                for ref, count in zip(got, CHUNKS):
                    part = ref[group * j : group * (j + 1), 0:count, z, low : low + SUB, :]
                    parts.append(part.reshape(group * count * SUB, lanes))
                halves.append(jnp.concatenate(parts, axis=0))
            tiles.append(jnp.concatenate(halves, axis=1))
        mean = sum(jnp.sum(t.astype(jnp.float32).reshape(frames, SUB, 2 * lanes), axis=0) for t in tiles)
        for i in range(len(tiles)):
            lowest = max(0, i - reach)
            rows = slice(i * width, (i + 1) * width)
            value = None
            for j in range(lowest, i + 1):
                low = (reach - i + j) * width
                part = dot(kernel_ref[:, low : low + width], tiles[j])
                value = part if value is None else value + part
            rowsum = rowsum_ref[rows, :].reshape(frames, SUB, lanes)
            value = value.reshape(frames, SUB, 2 * lanes)
            done = [
                value[:, :, h * lanes : (h + 1) * lanes] - rowsum * mean[None, :, h * lanes : (h + 1) * lanes]
                for h in range(2)
            ]
            both = jnp.concatenate(done, axis=1).astype(jnp.bfloat16)
            out_ref[i * frames : (i + 1) * frames, z, 2 * SUB * pair : 2 * SUB * (pair + 1), :] = both


def filter_frames(kernel, rowsum, got, total, group):
    owners, _, planes, strip, lanes = got[0].shape
    in_specs = [
        pl.BlockSpec(kernel.shape, lambda z: (0, 0)),
        pl.BlockSpec(rowsum.shape, lambda z: (0, 0)),
    ]
    for part in got:
        in_specs.append(pl.BlockSpec((owners, part.shape[1], 2, strip, lanes), lambda z: (0, 0, z, 0, 0)))

    def body(*refs):
        filter_body(group, *refs)

    return pl.pallas_call(
        body,
        grid=(planes // 2,),
        in_specs=in_specs,
        out_specs=pl.BlockSpec((total, 2, strip, lanes), lambda z: (0, z, 0, 0)),
        out_shape=jax.ShapeDtypeStruct((total, planes, strip, lanes), jnp.bfloat16),
        compiler_params=pltpu.CompilerParams(vmem_limit_bytes=VMEM),
        name="filter_frames",
    )(kernel, rowsum, *got)


def local(raw, offsets, taps):
    frame_dev, _, _, _ = raw.shape
    owners = lax.axis_size("frames")
    tiles = lax.axis_size("tiles")
    total = frame_dev * owners
    group = min(owners, 4)

    first_columns, last_columns = pack_edges(raw)
    upward = [(i, i + 1) for i in range(tiles - 1)]
    left = lax.ppermute(last_columns, "tiles", upward)
    right = lax.ppermute(first_columns, "tiles", [(j, i) for i, j in upward])

    tile = lax.axis_index("tiles")
    ends = jnp.stack([tile == 0, tile == tiles - 1]).astype(jnp.int32)
    meta = jnp.concatenate([offsets.reshape(-1), ends])

    order = []
    low = 0
    for count in CHUNKS:
        for owner in range(group):
            order += [owner * frame_dev + low + f for f in range(count)]
        low += count
    frames = group * frame_dev
    reach = min(-(-TAPS // frames), owners // group - 1)
    order = jnp.array(order + [1 << 20] * frames, jnp.int32)
    kernel, rowsum = spread_kernel(taps, jnp.tile(order[None], (SUB, 1)), total, frames, reach)

    got = []
    low = 0
    for count in CHUNKS:
        sent = register(raw, left, right, meta, low, count, owners)
        got.append(lax.all_to_all(sent, "frames", split_axis=0, concat_axis=0, tiled=True))
        low += count
    template = summed_over_frames(frame_sum(raw, left, right, meta), owners) * (1.0 / total)
    return filter_frames(kernel, rowsum, got, total, group), template


def summed_over_frames(value, owners):
    planes, rows, lanes = value.shape
    chips = owners // 2
    value = value.reshape(planes, chips, 2, rows // owners, lanes)
    index = lax.axis_index("frames")
    chip, core = lax.shift_right_logical(index, 1), lax.bitwise_and(index, 1)

    def block(array, axis, at):
        return lax.dynamic_index_in_dim(array, at, axis, keepdims=False)

    other = lax.ppermute(block(value, 2, 1 - core), "frames", [(i, i ^ 1) for i in range(owners)])
    value = block(value, 2, core) + other
    whole = block(value, 1, chip)
    for turn in range(1, chips):
        to = lax.bitwise_and(chip + turn, chips - 1)
        sent = block(value, 1, to).astype(jnp.bfloat16)
        other = lax.ppermute(sent, "frames", [(i, (i + 2 * turn) % owners) for i in range(owners)])
        whole = whole + other.astype(jnp.float32)
    return whole


def solution(mesh):
    placed = (P("frames", None, None, "tiles"), P("frames", None), P())
    return jax.shard_map(
        local,
        mesh=mesh,
        in_specs=placed,
        out_specs=(P(None, None, "frames", "tiles"), P(None, "frames", "tiles")),
        check_vma=False,
    )
```
